32 devices in a mesh: section: 2 (over x), dp: 16 (over z, y, core).
Axes of the slice: x: 2, y: 2, z: 4, core: 2. Of those that a mesh axis runs over, the one named last changes fastest.
Arguments:
- section_inputs: bfloat16 [2, 32, 128, 1024], P('section', 'dp'), may hold values from -4 to 4
- patch_index: int32 [32, 128], P('dp'), may hold values from 0 to 32767
- w_qkv: bfloat16 [2, 1024, 3072], P('section', 'dp'), may hold values from -1 to 1
- w_out: bfloat16 [2, 1024, 1024], P('section', 'dp'), may hold values from -0.1875 to 0.1875
- out_cotangent: bfloat16 [32, 128, 1024], P('dp'), may hold values from -6 to 6
Outputs:
- in_cotangent: bfloat16 [2, 32, 128, 1024], P('section', 'dp')
- grad_out: float32 [2, 1024, 1024], P('section', 'dp')
The draws below stay inside these ranges and needn't reach their ends.
All inputs are finite; a program needn't handle non-finite values.
Results may differ from the reference program's by a relative error of at most 0.034.
Values may be sent and summed in bfloat16 or wider, within the bound.
No kernel may reach another device: no remote copies, remote signals or barrier semaphores. Data moves between devices by JAX's collectives and lax.ppermute only.
A program may use at most 64 MiB of HBM per device.

```python
import math
import jax
import jax.numpy as jnp
from jax import lax

D = 1024
HEADS = 8
HD = 128
L = 128
GRID = 32
HW = 1024
PATCHES = 32768
SEQS = 32
TOKENS = 4096
N_SECTION = 2


def draw_section_inputs(key, part):
    full_shape = (N_SECTION, SEQS, L, D)
    base = jax.random.normal(key, full_shape, jnp.float32)
    return jnp.clip(base, -4.0, 4.0).astype(jnp.bfloat16)


def draw_w_qkv(key, part):
    base = jnp.clip(jax.random.normal(key, (N_SECTION, D, 3, HEADS, HD), jnp.float32), -4.0, 4.0) * D ** (-0.5)
    spread = jax.random.uniform(jax.random.fold_in(key, 11), (N_SECTION, 1, HEADS, 1), jnp.float32)
    head_scale = jnp.exp(math.log(0.8) + spread * math.log(2.5))
    query_part = base[:, :, 0] * head_scale
    key_part = base[:, :, 1] * head_scale
    stacked = jnp.stack([query_part, key_part, base[:, :, 2]], axis=2)
    return stacked.reshape(N_SECTION, D, 3 * HEADS * HD).astype(jnp.bfloat16)


def set_ends(entries, stream_key, low, largest):
    extent = entries.shape
    index_at = [jax.random.randint(jax.random.fold_in(stream_key, axis), (), 0, extent[axis]) for axis in range(len(extent))]
    entries = entries.at[tuple(index_at)].set(low)
    longest = extent.index(max(extent))
    index_at[longest] = (index_at[longest] + 1) % extent[longest]
    return entries.at[tuple(index_at)].set(largest)


def strengthened(array, rng, source, target, parts, factor):
    owner, partner = [(jnp.arange(array.shape[dim]) // (array.shape[dim] // parts)).reshape([-1 if axis == dim else 1 for axis in range(array.ndim)]) for dim in (source, target)]
    chosen = jax.random.permutation(rng, parts)[partner]
    strong = (owner == chosen) | (owner == (partner + parts // 2) % parts)
    return jnp.where(strong, factor * array, array)


def level_of(own_key, shape, cuts, least, high):
    factor_of, own = 1.0, jax.random.fold_in(own_key, 6)
    for dim, blocks in cuts:
        steps = jnp.exp(jax.random.uniform(jax.random.fold_in(own, dim), (blocks,), jnp.float32, least / len(cuts), high / len(cuts)))
        factor_of = factor_of * jnp.repeat(steps, shape[dim] // blocks).reshape([-1 if axis == dim else 1 for axis in range(len(shape))])
    return factor_of


def bell_draw(key, extent, width, bound, cuts=(), kind=jnp.bfloat16):
    values = width * jax.random.normal(key, extent, jnp.float32)
    if cuts:
        values = values * level_of(key, extent, cuts, -0.22, 0.18)
    return jnp.clip(values, -bound, bound).astype(kind)


def noise_with(own_key, dims, scale, most, shards, heavy, kind=jnp.bfloat16):
    entries = scale * jax.random.normal(own_key, dims, jnp.float32)
    if shards:
        entries = entries * level_of(own_key, dims, shards, -0.22, 0.18)
    return jnp.clip(strengthened(entries, jax.random.fold_in(own_key, 3), *heavy), -most, most).astype(kind)


def setup_inputs(seed: int = 0) -> dict:
    seeds = jax.random.split(jax.random.key(seed), 6)
    section_inputs = draw_section_inputs(jax.random.fold_in(seeds[5], 71), 0)
    patch_index = set_ends(jax.random.randint(seeds[1], (SEQS, L), 0, PATCHES), jax.random.fold_in(seeds[1], 1), 0, PATCHES - 1).astype(jnp.int32)
    w_qkv = draw_w_qkv(jax.random.fold_in(seeds[5], 71), 0)
    w_out = bell_draw(seeds[3], (N_SECTION, D, HW), HW ** -0.5, 0.1875, ((0, 2), (1, 16)))
    out_cotangent = noise_with(seeds[4], (SEQS, L, D), 1.0, 6.0, ((0, 16),), (0, 2, 16, 2.0))
    return dict(section_inputs=section_inputs, patch_index=patch_index, w_qkv=w_qkv, w_out=w_out, out_cotangent=out_cotangent)


def rotation_tables(patch_index):
    pair_count = HD // 2
    per_axis = (pair_count + 2) // 3
    grid_pos = jnp.stack([patch_index // (GRID * GRID), patch_index // GRID % GRID, patch_index % GRID], axis=-1).astype(jnp.float32)
    slot_ids = jnp.arange(pair_count, dtype=jnp.int32)
    picker = (slot_ids[:, None] % 3 == jnp.arange(3, dtype=jnp.int32)[None, :]).astype(jnp.float32)
    coords = jnp.einsum('nla,pa->nlp', grid_pos, picker, precision=lax.Precision.HIGHEST)
    freq_rates = jnp.power(10000.0, -(slot_ids // 3).astype(jnp.float32) / per_axis)
    angles = coords * freq_rates
    return (jnp.cos(angles)[:, :, None, :], jnp.sin(angles)[:, :, None, :])

def rotate(tensor, cosine_tab, sine_tab):
    half_width = tensor.shape[-1] // 2
    first_half = tensor[..., :half_width]
    second_half = tensor[..., half_width:]
    return jnp.concatenate([first_half * cosine_tab - second_half * sine_tab, first_half * sine_tab + second_half * cosine_tab], axis=-1)

def lowered(tensor):
    return lax.optimization_barrier(tensor.astype(jnp.bfloat16)).astype(jnp.float32)

def section_backward(inputs, qkv_weight, out_weight, cosine_tab, sine_tab, incoming):
    seq_count, length, model_width = inputs.shape
    attn_width = HEADS * HD
    inputs_f = inputs.astype(jnp.float32)
    inv_rms = lax.rsqrt(lax.optimization_barrier(jnp.mean(inputs_f * inputs_f, axis=-1, keepdims=True)) + 1e-06)
    normed = (inputs_f * inv_rms).astype(jnp.bfloat16)
    projected = jnp.dot(normed.reshape(seq_count * length, model_width), qkv_weight, preferred_element_type=jnp.float32)
    split_heads = projected.reshape(seq_count, length, 3, HEADS, HD)
    queries = lowered(rotate(split_heads[:, :, 0], cosine_tab, sine_tab))
    key_rows = lowered(rotate(split_heads[:, :, 1], cosine_tab, sine_tab))
    values = lowered(split_heads[:, :, 2])
    scores = jnp.einsum('nqhe,nkhe->nhqk', queries, key_rows) * HD ** (-0.5)
    attn_probs = jax.nn.softmax(scores, axis=-1)
    probs_low = lowered(attn_probs)
    mixed_heads = jnp.einsum('nhqk,nkhe->nqhe', probs_low, values).astype(jnp.bfloat16)
    cot_rows = incoming.reshape(seq_count * length, model_width)
    grad_term = jnp.dot(cot_rows.T, mixed_heads.reshape(seq_count * length, attn_width), preferred_element_type=jnp.float32)
    grad_mixed = lowered(jnp.dot(cot_rows, out_weight, preferred_element_type=jnp.float32)).reshape(seq_count, length, HEADS, HD)
    grad_probs = jnp.einsum('nqhe,nkhe->nhqk', grad_mixed, values)
    grad_values = jnp.einsum('nhqk,nqhe->nkhe', probs_low, grad_mixed).astype(jnp.bfloat16)
    grad_scores = lowered(attn_probs * (grad_probs - lax.optimization_barrier(jnp.sum(grad_probs * attn_probs, axis=-1, keepdims=True))) * HD ** (-0.5))
    grad_query = rotate(jnp.einsum('nhqk,nkhe->nqhe', grad_scores, key_rows), cosine_tab, -sine_tab).astype(jnp.bfloat16)
    grad_keys = rotate(jnp.einsum('nhqk,nqhe->nkhe', grad_scores, queries), cosine_tab, -sine_tab).astype(jnp.bfloat16)
    grad_proj = jnp.stack([grad_query, grad_keys, grad_values], axis=2).reshape(seq_count * length, 3 * attn_width)
    grad_normed = jnp.dot(grad_proj, qkv_weight.T, preferred_element_type=jnp.float32).reshape(seq_count, length, model_width)
    grad_inputs = incoming.astype(jnp.float32) + inv_rms * grad_normed - inputs_f * inv_rms ** 3 * lax.optimization_barrier(jnp.mean(grad_normed * inputs_f, axis=-1, keepdims=True))
    return (grad_inputs.astype(jnp.bfloat16), grad_term)

def reference(section_inputs, patch_index, w_qkv, w_out, out_cotangent):
    cosine_tab, sine_tab = rotation_tables(patch_index)
    incoming = out_cotangent
    cot_list = [None] * N_SECTION
    grad_list = [None] * N_SECTION
    for section_num in range(N_SECTION - 1, -1, -1):
        grad_inputs, grad_term = section_backward(section_inputs[section_num], w_qkv[section_num], w_out[section_num], cosine_tab, sine_tab, incoming)
        cot_list[section_num] = grad_inputs
        grad_list[section_num] = grad_term * TOKENS ** (-0.5)
        incoming = grad_inputs
    return (jnp.stack(cot_list), jnp.stack(grad_list))
```

```python
import functools

import jax
import jax.numpy as jnp
import numpy as np
from jax import lax
from jax.experimental import pallas as pl
from jax.experimental.pallas import tpu as pltpu
from jax.sharding import PartitionSpec as P

HEADS = 8
HD = 128
GRID = 32
WIDTH = HEADS * HD
SCALE = HD**-0.5
F32 = jnp.float32
BF16 = jnp.bfloat16
VMEM_LIMIT = 48 * 1024 * 1024


def ring_pairs(chips, step):
    order = [2 * r if r < chips // 2 else 2 * (chips - 1 - r) + 1 for r in range(chips)]
    return [
        (2 * order[r] + core, 2 * order[(r + step) % chips] + core)
        for r in range(chips)
        for core in range(2)
    ]


def chip_at(me, offset, chips):
    chip = me // 2
    place = jnp.where(chip % 2 == 0, chip // 2, chips - 1 - chip // 2)
    there = (place + (offset + chips)) % chips
    return jnp.where(there < chips // 2, 2 * there, 2 * (chips - 1 - there) + 1)


def swap_cores(value, dp_count):
    return lax.ppermute(value, "dp", [(i, i ^ 1) for i in range(dp_count)])


def in_hbm(value):
    return pltpu.with_memory_space_constraint(value, pltpu.HBM)


def gather_rows(shards, dp_count):
    chips = dp_count // 2
    far = chips // 2
    ahead, behind = ring_pairs(chips, 1), ring_pairs(chips, -1)
    pieces = [[shard] for shard in shards]
    places = [[(0, 0, 0)] for _ in shards]
    ends = [(shard, shard) for shard in shards]

    def advance(number, hop):
        up, down = ends[number]
        half = up.shape[0] // 2
        if hop == far:
            up, down = up[:half], down[half:]
        up = lax.ppermute(up, "dp", ahead)
        down = lax.ppermute(down, "dp", behind)
        ends[number] = (up, down)
        pieces[number] += [up, down]
        places[number] += [(-hop, 0, 0), (hop, 0, half if hop == far else 0)]

    for step in range(1, far + len(shards)):
        for number in range(len(shards)):
            if 1 <= step - number <= far:
                if number:
                    ends[:] = lax.optimization_barrier(ends)
                advance(number, step - number)
    pieces = [[in_hbm(value) for value in one] for one in pieces]
    for number in range(len(shards)):
        places[number] += [(offset, 1, row) for offset, _, row in places[number]]
        pieces[number] += [in_hbm(swap_cores(value, dp_count)) for value in pieces[number]]
    return pieces, places


def start_rows(refs, places, chips, me, target, sems):
    copies = []
    for number, (ref, place) in enumerate(zip(refs, places)):
        rows = ref.shape[0]
        if place is None:
            into = target
        else:
            offset, other, low = place
            owner = 2 * chip_at(me, offset, chips) + lax.rem(me + other, 2)
            row = pl.multiple_of(owner * (target.shape[0] // (2 * chips)) + low, rows)
            into = target.at[pl.ds(row, rows)]
        copy = pltpu.make_async_copy(ref, into, sems.at[number])
        copy.start()
        copies.append(copy)
    return copies


def turn(value, cosine, sine):
    return value * cosine + pltpu.roll(value, HD // 2, 1) * sine


def rms_of(inputs_f):
    return lax.rsqrt(jnp.mean(inputs_f * inputs_f, axis=-1, keepdims=True) + 1e-06)


def dot_nt(a, b):
    return lax.dot_general(a, b, (((1,), (1,)), ((), ())), preferred_element_type=F32)


def dot_tn(a, b):
    return lax.dot_general(a, b, (((0,), (0,)), ((), ())), preferred_element_type=F32)


def forward_kernel(places, chips, seqs, length, facts, x, cosine, sine, *rest):
    count = len(places)
    pieces = rest[:count]
    queries, key_rows, values, probs, mixed = rest[count : count + 5]
    weights, normed, sems = rest[count + 5 :]
    copies = start_rows(pieces, places, chips, facts[0], weights, sems)
    x_f = x[...].astype(F32)
    normed[...] = (x_f * rms_of(x_f)).astype(BF16)
    for copy in copies:
        copy.wait()
    for pair in range(HEADS // 2):
        column = pair * 2 * HD
        blocks = [
            jnp.dot(
                normed[...],
                weights[:, part * WIDTH + column : part * WIDTH + column + 2 * HD],
                preferred_element_type=F32,
            )
            for part in range(3)
        ]
        for head in range(2):
            here = slice(head * HD, head * HD + HD)
            there = slice(column + head * HD, column + head * HD + HD)
            q = turn(blocks[0][:, here], cosine[...], sine[...]).astype(BF16)
            k = turn(blocks[1][:, here], cosine[...], sine[...]).astype(BF16)
            v = blocks[2][:, here].astype(BF16)
            queries[:, there] = q
            key_rows[:, there] = k
            values[:, there] = v
            for seq in range(seqs):
                rows = slice(seq * length, seq * length + length)
                scores = dot_nt(q[rows], k[rows]) * SCALE
                raised = jnp.exp(scores - jnp.max(scores, axis=-1, keepdims=True))
                prob = raised * (1.0 / jnp.sum(raised, axis=-1, keepdims=True))
                probs[(2 * pair + head) * seqs + seq] = prob
                mixed[rows, there] = jnp.dot(
                    prob.astype(BF16), v[rows], preferred_element_type=F32
                ).astype(BF16)


def backward_kernel(
    places_in, places_out, chips, seqs, length, first,
    facts, incoming, previous, x, cosine, sine, queries, key_rows, values, probs, *rest,
):
    count_in, count_out = len(places_in), len(places_out)
    pieces_in = rest[:count_in]
    pieces_out = rest[count_in : count_in + count_out]
    grad_inputs = rest[count_in + count_out]
    w_in, w_out, grad_mixed, grad_proj, grad_normed, sems_in, sems_out = rest[
        count_in + count_out + 1 :
    ]

    @pl.when(facts[1] != 0)
    def _():
        copies_out = start_rows(pieces_out, places_out, chips, facts[0], w_out, sems_out)
        copies_in = start_rows(pieces_in, places_in, chips, facts[0], w_in, sems_in)
        for copy in copies_out:
            copy.wait()
        for pair in range(HEADS // 2):
            column = pair * 2 * HD
            grad_mixed[:, column : column + 2 * HD] = jnp.dot(
                incoming[...], w_out[:, column : column + 2 * HD], preferred_element_type=F32
            ).astype(BF16)
        for head in range(HEADS):
            there = slice(head * HD, head * HD + HD)
            for seq in range(seqs):
                rows = slice(seq * length, seq * length + length)
                prob = probs[head * seqs + seq]
                g_mixed = grad_mixed[rows, there]
                grad_probs = dot_nt(g_mixed, values[rows, there])
                grad_values = dot_tn(prob.astype(BF16), g_mixed)
                weighted = grad_probs * prob
                grad_scores = (
                    prob * (grad_probs - jnp.sum(weighted, axis=-1, keepdims=True)) * SCALE
                ).astype(BF16)
                grad_q = jnp.dot(grad_scores, key_rows[rows, there], preferred_element_type=F32)
                grad_k = dot_tn(grad_scores, queries[rows, there])
                low = seq * length
                grad_proj[rows, head * HD : head * HD + HD] = turn(
                    grad_q, cosine[low : low + length], -sine[low : low + length]
                ).astype(BF16)
                grad_proj[rows, WIDTH + head * HD : WIDTH + head * HD + HD] = turn(
                    grad_k, cosine[low : low + length], -sine[low : low + length]
                ).astype(BF16)
                grad_proj[rows, 2 * WIDTH + head * HD : 2 * WIDTH + head * HD + HD] = (
                    grad_values.astype(BF16)
                )
        for copy in copies_in:
            copy.wait()
        width = x.shape[1]
        for low in range(0, width, 256):
            grad_normed[:, low : low + 256] = dot_nt(grad_proj[...], w_in[low : low + 256, :])
        x_f = x[...].astype(F32)
        inv_rms = rms_of(x_f)
        g_normed = grad_normed[...]
        shift = jnp.mean(g_normed * x_f, axis=-1, keepdims=True)
        grad_inputs[...] = (
            incoming[...].astype(F32) + inv_rms * g_normed - x_f * (inv_rms**3 * shift)
        ).astype(BF16)

    @pl.when(facts[1] == 0)
    def _():
        grad_inputs[...] = incoming[...] if first else previous[...]


def term_kernel(chips, facts, incoming, mixed, mine, others):
    me = facts[0]
    width = incoming.shape[1]
    rows = width // (2 * chips)
    upper = lax.rem(me, 2) == 0
    for offset in range(chips):
        chip = chip_at(me, offset, chips)
        column = pl.multiple_of(chip * 2 * rows, 2 * rows)
        term = dot_tn(incoming[:, pl.ds(column, 2 * rows)], mixed[...])
        first, second = term[:rows], term[rows:]
        mine[offset] = jnp.where(upper, first, second).astype(BF16)
        others[offset] = jnp.where(upper, second, first).astype(BF16)


def sum_rows(mine, others, dp_count, tied):
    chips = dp_count // 2
    ahead, behind = ring_pairs(chips, 1), ring_pairs(chips, -1)
    from_core = swap_cores(others, dp_count)

    def held(offset, columns=slice(None)):
        return mine[offset, :, columns].astype(F32) + from_core[offset, :, columns].astype(F32)

    half = mine.shape[2] // 2
    far = chips // 2
    low, high = slice(None, half), slice(half, None)
    up = lax.ppermute(held(far, low).astype(BF16), "dp", ahead)
    down = lax.ppermute(held(far, high).astype(BF16), "dp", behind)
    blank = jnp.zeros_like(up)
    up, down = jnp.concatenate([up, blank], 1), jnp.concatenate([blank, down], 1)
    for hop in range(far - 1, 0, -1):
        up = lax.ppermute((held(hop) + up.astype(F32)).astype(BF16), "dp", ahead)
        down = lax.ppermute((held(chips - hop) + down.astype(F32)).astype(BF16), "dp", behind)
        if hop == far - 1:
            up, down, tied = lax.optimization_barrier((up, down, tied))
    return held(0) + up.astype(F32) + down.astype(F32), tied


def rotation_tables(patch_index):
    slots = np.arange(HD) % (HD // 2)
    per_axis = (HD // 2 + 2) // 3
    rates = jnp.asarray(np.power(10000.0, -(slots // 3) / per_axis), F32)
    axis = jnp.asarray(slots % 3, jnp.int32)
    index = patch_index.reshape(-1, 1)
    places = jnp.where(
        axis == 0, index // (GRID * GRID), jnp.where(axis == 1, index // GRID % GRID, index % GRID)
    )
    angles = places.astype(F32) * rates
    signs = jnp.asarray(np.where(np.arange(HD) < HD // 2, -1.0, 1.0), F32)
    return jnp.cos(angles), jnp.sin(angles) * signs


def per_device(section_inputs, patch_index, w_qkv, w_out, out_cotangent):
    seqs, length, width = section_inputs.shape[1:]
    tokens = seqs * length
    sections = lax.axis_size("section")
    dp_count = lax.axis_size("dp")
    chips = dp_count // 2
    by_ring = dp_count % 4 == 0 and 4 <= chips <= 8
    dp_idx = lax.axis_index("dp").astype(jnp.int32)
    section_idx = lax.axis_index("section")
    x = section_inputs[0].reshape(tokens, width)
    cosine, sine = rotation_tables(patch_index)
    if by_ring:
        (in_pieces, out_pieces), (in_places, out_places) = gather_rows(
            [w_qkv[0], w_out[0]], dp_count
        )
    else:
        in_pieces = [lax.all_gather(w_qkv[0], "dp", axis=0, tiled=True)]
        out_pieces = [lax.all_gather(w_out[0], "dp", axis=0, tiled=True)]
        in_places, out_places = [None], [None]

    smem = pl.BlockSpec(memory_space=pltpu.SMEM)
    vmem = pl.BlockSpec(memory_space=pltpu.VMEM)
    anywhere = pl.BlockSpec(memory_space=pltpu.HBM)
    params = pltpu.CompilerParams(vmem_limit_bytes=VMEM_LIMIT)
    like = jax.ShapeDtypeStruct((tokens, width), BF16)
    heads_like = jax.ShapeDtypeStruct((tokens, WIDTH), BF16)

    queries, key_rows, values, probs, mixed = pl.pallas_call(
        functools.partial(forward_kernel, in_places, chips, seqs, length),
        out_shape=[heads_like] * 3
        + [jax.ShapeDtypeStruct((HEADS * seqs, length, length), F32), heads_like],
        in_specs=[smem, vmem, vmem, vmem] + [anywhere] * len(in_pieces),
        out_specs=[vmem] * 5,
        scratch_shapes=[
            pltpu.VMEM((width, 3 * WIDTH), BF16),
            pltpu.VMEM((tokens, width), BF16),
            pltpu.SemaphoreType.DMA((len(in_pieces),)),
        ],
        compiler_params=params,
        cost_estimate=pl.CostEstimate(
            flops=2 * tokens * width * 3 * WIDTH,
            bytes_accessed=6 * width * WIDTH,
            transcendentals=0,
        ),
        name="forward",
    )(jnp.stack([dp_idx, dp_idx]), x, cosine, sine, *in_pieces)
    mixed_above = lax.ppermute(mixed, "section", [(s, (s + 1) % sections) for s in range(sections)])

    def stage(number, incoming, previous):
        active = (section_idx == sections - 1 - number).astype(jnp.int32)
        return pl.pallas_call(
            functools.partial(
                backward_kernel, in_places, out_places, chips, seqs, length, number == 0
            ),
            out_shape=like,
            in_specs=[smem] + [vmem] * 9 + [anywhere] * (len(in_pieces) + len(out_pieces)),
            out_specs=vmem,
            scratch_shapes=[
                pltpu.VMEM((width, 3 * WIDTH), BF16),
                pltpu.VMEM((width, WIDTH), BF16),
                pltpu.VMEM((tokens, WIDTH), BF16),
                pltpu.VMEM((tokens, 3 * WIDTH), BF16),
                pltpu.VMEM((tokens, width), F32),
                pltpu.SemaphoreType.DMA((len(in_pieces),)),
                pltpu.SemaphoreType.DMA((len(out_pieces),)),
            ],
            compiler_params=params,
            cost_estimate=pl.CostEstimate(
                flops=2 * tokens * width * 4 * WIDTH,
                bytes_accessed=8 * width * WIDTH,
                transcendentals=0,
            ),
            name="backward",
        )(
            jnp.stack([dp_idx, active]), incoming, previous, x, cosine, sine,
            queries, key_rows, values, probs, *in_pieces, *out_pieces,
        )

    carried = out_cotangent.reshape(tokens, width)
    incoming = carried
    back = [(s, s - 1) for s in range(1, sections)]
    for number in range(sections - 1):
        carried = stage(number, incoming, carried)
        incoming = lax.ppermute(carried, "section", back)
    ready = carried

    if by_ring:
        block = jax.ShapeDtypeStruct((chips, width // dp_count, WIDTH), BF16)
        mine, others = pl.pallas_call(
            functools.partial(term_kernel, chips),
            out_shape=[block, block],
            in_specs=[smem, vmem, vmem],
            out_specs=[vmem, vmem],
            compiler_params=params,
            cost_estimate=pl.CostEstimate(
                flops=2 * tokens * width * WIDTH,
                bytes_accessed=2 * width * WIDTH,
                transcendentals=0,
            ),
            name="term",
        )(jnp.stack([dp_idx, dp_idx]), ready, mixed_above)
        grad_sum, incoming = sum_rows(mine, others, dp_count, incoming)
    else:
        grad_sum = lax.psum_scatter(
            dot_tn(ready, mixed_above), "dp", scatter_dimension=0, tiled=True
        )
    carried = stage(sections - 1, incoming, carried)
    grad_sum = lax.ppermute(
        grad_sum.astype(BF16), "section", [(s, (s - 1) % sections) for s in range(sections)]
    )
    grad_sum = grad_sum.astype(F32) * float(tokens * dp_count) ** (-0.5)
    return carried.reshape(1, seqs, length, width), grad_sum[None]


def solution(mesh):
    in_specs = (
        P("section", "dp", None, None),
        P("dp", None),
        P("section", "dp", None),
        P("section", "dp", None),
        P("dp", None, None),
    )
    out_specs = (P("section", "dp", None, None), P("section", "dp", None))
    return jax.shard_map(
        per_device, mesh=mesh, in_specs=in_specs, out_specs=out_specs, check_vma=False
    )
```

```python
import functools

import jax
import jax.numpy as jnp
import numpy as np
from jax import lax
from jax.experimental import pallas as pl
from jax.experimental.pallas import tpu as pltpu
from jax.sharding import PartitionSpec as P

HEADS = 8
HD = 128
GRID = 32
WIDTH = HEADS * HD
SCALE = HD**-0.5
F32 = jnp.float32
BF16 = jnp.bfloat16
VMEM_LIMIT = 48 * 1024 * 1024


def ring_pairs(chips, step):
    order = [2 * r if r < chips // 2 else 2 * (chips - 1 - r) + 1 for r in range(chips)]
    return [
        (2 * order[r] + core, 2 * order[(r + step) % chips] + core)
        for r in range(chips)
        for core in range(2)
    ]


def chip_at(me, offset, chips):
    chip = me // 2
    place = jnp.where(chip % 2 == 0, chip // 2, chips - 1 - chip // 2)
    there = (place + (offset + chips)) % chips
    return jnp.where(there < chips // 2, 2 * there, 2 * (chips - 1 - there) + 1)


def swap_cores(value, dp_count):
    return lax.ppermute(value, "dp", [(i, i ^ 1) for i in range(dp_count)])


def in_hbm(value):
    return pltpu.with_memory_space_constraint(value, pltpu.HBM)


def gather_rows(shard, tables, dp_count):
    chips = dp_count // 2
    far = chips // 2
    half = shard.shape[0] // 2
    ahead, behind = ring_pairs(chips, 1), ring_pairs(chips, -1)
    up = down = shard
    pieces = [(shard, 0, 0, 0)]
    for hop in range(1, far):
        up = lax.ppermute(up, "dp", ahead)
        down = lax.ppermute(down, "dp", behind)
        if hop == 1:
            down, tables = lax.optimization_barrier((down, tables))
        pieces += [(up, -hop, 0, 0), (down, hop, 0, 0)]
    up = lax.ppermute(up[:half], "dp", ahead)
    down = lax.ppermute(down[half:], "dp", behind)
    pieces += [(up, -far, 0, 0), (down, far, 0, half)]
    pieces = [(in_hbm(value), *place) for value, *place in pieces]
    pieces += [
        (in_hbm(swap_cores(value, dp_count)), offset, 1, row) for value, offset, _, row in pieces
    ]
    return [piece[0] for piece in pieces], [piece[1:] for piece in pieces], tables


def start_rows(pieces, places, chips, me, columns, target, sems):
    copies = []
    per_owner = target.shape[0] // (2 * chips)
    for number, (piece, place) in enumerate(zip(pieces, places)):
        rows = piece.shape[0]
        into = target
        if place is not None:
            offset, other, low = place
            owner = 2 * chip_at(me, offset, chips) + lax.rem(me + other, 2)
            into = target.at[pl.ds(pl.multiple_of(owner * per_owner + low, rows), rows)]
        copy = pltpu.make_async_copy(piece.at[:, columns], into, sems.at[number])
        copy.start()
        copies.append(copy)
    return copies


def head_spots(seqs, length):
    return [
        (slice(seq * length, seq * length + length), slice(head * HD, head * HD + HD))
        for head in range(HEADS)
        for seq in range(seqs)
    ]


def turn(value, cosine, sine):
    return value * cosine + pltpu.roll(value, HD // 2, 1) * sine


def rms_of(inputs_f):
    return lax.rsqrt(jnp.mean(inputs_f * inputs_f, axis=-1, keepdims=True) + 1e-06)


def dot_nt(a, b):
    return lax.dot_general(a, b, (((1,), (1,)), ((), ())), preferred_element_type=F32)


def dot_tn(a, b):
    return lax.dot_general(a, b, (((0,), (0,)), ((), ())), preferred_element_type=F32)


def forward_kernel(places, chips, seqs, length, facts, x, cosine, sine, *rest):
    count = len(places)
    queries, key_rows, values, probs, mixed, weights, normed, sems = rest[count:]
    copies = start_rows(
        rest[:count], places, chips, facts[0], pl.ds(0, 3 * WIDTH), weights, sems
    )
    x_f = x[...].astype(F32)
    normed[...] = (x_f * rms_of(x_f)).astype(BF16)
    for copy in copies:
        copy.wait()
    for part, target in enumerate((queries, key_rows, values)):
        for column in range(0, WIDTH, 2 * HD):
            low = part * WIDTH + column
            block = jnp.dot(
                normed[...], weights[:, low : low + 2 * HD], preferred_element_type=F32
            )
            for head in range(2):
                one = block[:, head * HD : head * HD + HD]
                if part < 2:
                    one = turn(one, cosine[...], sine[...])
                target[:, column + head * HD : column + head * HD + HD] = one.astype(BF16)
    spots = head_spots(seqs, length)
    scores = [dot_nt(queries[spot], key_rows[spot]) * SCALE for spot in spots]
    highest = [jnp.max(one, axis=-1, keepdims=True) for one in scores]
    raised = [jnp.exp(one - top) for one, top in zip(scores, highest)]
    totals = [jnp.sum(one, axis=-1, keepdims=True) for one in raised]
    each = [one * (1.0 / total) for one, total in zip(raised, totals)]
    for number, prob in enumerate(each):
        probs[number] = prob
    for spot, prob in zip(spots, each):
        mixed[spot] = jnp.dot(
            prob.astype(BF16), values[spot], preferred_element_type=F32
        ).astype(BF16)


def copy_rows(sources, targets):
    rows = min(ref.shape[0] for ref in (*sources, *targets))
    for low in range(0, sum(ref.shape[0] for ref in sources), rows):
        source, target = (refs[low // refs[0].shape[0]] for refs in (sources, targets))
        here, there = low % source.shape[0], low % target.shape[0]
        target[there : there + rows] = source[here : here + rows]


def backward_kernel(
    places, chips, seqs, length, counts, first, facts, x, cosine, sine, queries, key_rows, values,
    probs, *rest,
):
    groups = []
    for count in (counts[0], counts[1], len(places)):
        groups.append(rest[:count])
        rest = rest[count:]
    arrived, previous, outs, pieces = groups[0], groups[1], rest[: counts[2]], groups[2]
    incoming, w_in, w_out, grad_mixed, grad_proj, grad_normed, sems_in, sems_out = rest[
        counts[2] :
    ]

    @pl.when(facts[1] != 0)
    def _():
        me = facts[0]
        copies_out = start_rows(
            pieces, places, chips, me, pl.ds(3 * WIDTH, WIDTH), w_out, sems_out
        )
        copies_in = start_rows(pieces, places, chips, me, pl.ds(0, 3 * WIDTH), w_in, sems_in)
        copy_rows(arrived, [incoming])
        for copy in copies_out:
            copy.wait()
        for column in range(0, WIDTH, 2 * HD):
            grad_mixed[:, column : column + 2 * HD] = jnp.dot(
                incoming[...], w_out[:, column : column + 2 * HD], preferred_element_type=F32
            ).astype(BF16)
        spots = head_spots(seqs, length)
        each = [probs[number] for number in range(len(spots))]
        grad_probs = [dot_nt(grad_mixed[spot], values[spot]) for spot in spots]
        grad_values = [
            dot_tn(prob.astype(BF16), grad_mixed[spot]) for prob, spot in zip(each, spots)
        ]
        shifts = [
            jnp.sum(grad * prob, axis=-1, keepdims=True) for grad, prob in zip(grad_probs, each)
        ]
        grad_scores = [
            (prob * (grad - shift) * SCALE).astype(BF16)
            for prob, grad, shift in zip(each, grad_probs, shifts)
        ]
        grad_q = [
            jnp.dot(grad, key_rows[spot], preferred_element_type=F32)
            for grad, spot in zip(grad_scores, spots)
        ]
        grad_k = [dot_tn(grad, queries[spot]) for grad, spot in zip(grad_scores, spots)]
        for (rows, columns), one_q, one_k, one_v in zip(spots, grad_q, grad_k, grad_values):
            low = columns.start
            back = -sine[rows]
            grad_proj[rows, low : low + HD] = turn(one_q, cosine[rows], back).astype(BF16)
            low += WIDTH
            grad_proj[rows, low : low + HD] = turn(one_k, cosine[rows], back).astype(BF16)
            low += WIDTH
            grad_proj[rows, low : low + HD] = one_v.astype(BF16)
        for copy in copies_in:
            copy.wait()
        for low in range(0, x.shape[1], 256):
            grad_normed[:, low : low + 256] = dot_nt(grad_proj[...], w_in[low : low + 256, :])
        x_f = x[...].astype(F32)
        inv_rms = rms_of(x_f)
        g_normed = grad_normed[...]
        shift = jnp.mean(g_normed * x_f, axis=-1, keepdims=True)
        incoming[...] = (
            incoming[...].astype(F32) + inv_rms * g_normed - x_f * (inv_rms**3 * shift)
        ).astype(BF16)
        copy_rows([incoming], outs)

    @pl.when(facts[1] == 0)
    def _():
        copy_rows(arrived if first else previous, outs)


def term_kernel(chips, facts, *refs):
    *incoming, mixed, mine, others, others_far = refs
    me = facts[0]
    width = incoming[0].shape[1]
    rows = width // (2 * chips)
    upper = lax.rem(me, 2) == 0
    for offset in [chips // 2, *range(chips // 2), *range(chips // 2 + 1, chips)]:
        chip = chip_at(me, offset, chips)
        column = pl.multiple_of(chip * 2 * rows, 2 * rows)
        taken = [ref[:, pl.ds(column, 2 * rows)] for ref in incoming]
        term = dot_tn(jnp.concatenate(taken, axis=0), mixed[...])
        first, second = term[:rows], term[rows:]
        mine[offset] = jnp.where(upper, first, second).astype(BF16)
        other = jnp.where(upper, second, first).astype(BF16)
        if offset == chips // 2:
            others_far[...] = other
        else:
            others[offset - (offset > chips // 2)] = other


def sum_rows(mine, others, others_far, dp_count, tied):
    chips = dp_count // 2
    far = chips // 2
    ahead, behind = ring_pairs(chips, 1), ring_pairs(chips, -1)
    from_far = swap_cores(others_far, dp_count)
    from_core = swap_cores(others, dp_count)

    def held(offset, columns=slice(None)):
        more = from_far if offset == far else from_core[offset - (offset > far)]
        return mine[offset, :, columns].astype(F32) + more[:, columns].astype(F32)

    half = mine.shape[2] // 2
    low, high = slice(None, half), slice(half, None)
    up = lax.ppermute(held(far, low).astype(BF16), "dp", ahead)
    down = lax.ppermute(held(far, high).astype(BF16), "dp", behind)
    blank = jnp.zeros_like(up)
    up, down = jnp.concatenate([up, blank], 1), jnp.concatenate([blank, down], 1)
    tied = list(tied)
    up, down, tied[0] = lax.optimization_barrier((up, down, tied[0]))
    for hop in range(far - 1, 0, -1):
        if hop == 1:
            up, down, tied[-1] = lax.optimization_barrier((up, down, tied[-1]))
        up = lax.ppermute((held(hop) + up.astype(F32)).astype(BF16), "dp", ahead)
        down = lax.ppermute((held(chips - hop) + down.astype(F32)).astype(BF16), "dp", behind)
    return held(0) + up.astype(F32) + down.astype(F32), tied


def rotation_tables(patch_index):
    slots = np.arange(HD) % (HD // 2)
    per_axis = (HD // 2 + 2) // 3
    rates = jnp.asarray(np.power(10000.0, -(slots // 3) / per_axis), F32)
    axis = jnp.asarray(slots % 3, jnp.int32)
    index = patch_index.reshape(-1, 1)
    places = jnp.where(
        axis == 0, index // (GRID * GRID), jnp.where(axis == 1, index // GRID % GRID, index % GRID)
    )
    angles = places.astype(F32) * rates
    signs = jnp.asarray(np.where(np.arange(HD) < HD // 2, -1.0, 1.0), F32)
    return jnp.cos(angles), jnp.sin(angles) * signs


def per_device(section_inputs, patch_index, w_qkv, w_out, out_cotangent):
    seqs, length, width = section_inputs.shape[1:]
    tokens = seqs * length
    sections = lax.axis_size("section")
    dp_count = lax.axis_size("dp")
    chips = dp_count // 2
    by_ring = dp_count % 4 == 0 and 4 <= chips <= 8
    dp_idx = lax.axis_index("dp").astype(jnp.int32)
    section_idx = lax.axis_index("section")
    x = section_inputs[0].reshape(tokens, width)
    cosine, sine = rotation_tables(patch_index)
    shard = jnp.concatenate([w_qkv[0], w_out[0]], axis=1)
    if by_ring:
        pieces, places, (cosine, sine) = gather_rows(shard, (cosine, sine), dp_count)
    else:
        pieces, places = [lax.all_gather(shard, "dp", axis=0, tiled=True)], [None]

    smem = pl.BlockSpec(memory_space=pltpu.SMEM)
    vmem = pl.BlockSpec(memory_space=pltpu.VMEM)
    anywhere = pl.BlockSpec(memory_space=pltpu.HBM)
    params = pltpu.CompilerParams(vmem_limit_bytes=VMEM_LIMIT)
    like = jax.ShapeDtypeStruct((tokens, width), BF16)
    heads_like = jax.ShapeDtypeStruct((tokens, WIDTH), BF16)

    queries, key_rows, values, probs, mixed = pl.pallas_call(
        functools.partial(forward_kernel, places, chips, seqs, length),
        out_shape=[heads_like] * 3
        + [jax.ShapeDtypeStruct((HEADS * seqs, length, length), F32), heads_like],
        in_specs=[smem, vmem, vmem, vmem] + [anywhere] * len(pieces),
        out_specs=[vmem] * 5,
        scratch_shapes=[
            pltpu.VMEM((width, 3 * WIDTH), BF16),
            pltpu.VMEM((tokens, width), BF16),
            pltpu.SemaphoreType.DMA((len(pieces),)),
        ],
        compiler_params=params,
        cost_estimate=pl.CostEstimate(
            flops=2 * tokens * width * 3 * WIDTH,
            bytes_accessed=6 * width * WIDTH,
            transcendentals=0,
        ),
        name="forward",
    )(jnp.stack([dp_idx, dp_idx]), x, cosine, sine, *pieces)
    values = in_hbm(values)
    mixed_above = lax.ppermute(mixed, "section", [(s, (s + 1) % sections) for s in range(sections)])

    def stage(number, incoming, previous):
        active = (section_idx == sections - 1 - number).astype(jnp.int32)
        parts = 1 if number == sections - 1 else 2
        counts = (len(incoming), len(previous), parts)
        return pl.pallas_call(
            functools.partial(backward_kernel, places, chips, seqs, length, counts, number == 0),
            out_shape=[jax.ShapeDtypeStruct((tokens // parts, width), BF16)] * parts,
            in_specs=[smem]
            + [vmem] * (7 + len(incoming) + len(previous))
            + [anywhere] * len(pieces),
            out_specs=[vmem] * parts,
            scratch_shapes=[
                pltpu.VMEM((tokens, width), BF16),
                pltpu.VMEM((width, 3 * WIDTH), BF16),
                pltpu.VMEM((width, WIDTH), BF16),
                pltpu.VMEM((tokens, WIDTH), BF16),
                pltpu.VMEM((tokens, 3 * WIDTH), BF16),
                pltpu.VMEM((tokens, width), F32),
                pltpu.SemaphoreType.DMA((len(pieces),)),
                pltpu.SemaphoreType.DMA((len(pieces),)),
            ],
            compiler_params=params,
            cost_estimate=pl.CostEstimate(
                flops=2 * tokens * width * 4 * WIDTH,
                bytes_accessed=8 * width * WIDTH,
                transcendentals=0,
            ),
            name="backward",
        )(
            jnp.stack([dp_idx, active]), x, cosine, sine, queries, key_rows, values, probs,
            *incoming, *previous, *pieces,
        )

    carried = [out_cotangent.reshape(tokens, width)]
    incoming, previous = carried, []
    back = [(s, s - 1) for s in range(1, sections)]
    for number in range(sections - 1):
        carried = stage(number, incoming, previous)
        incoming = [lax.ppermute(value, "section", back) for value in carried]
        previous = carried
    ready = carried

    if by_ring:
        mine, others, others_far = pl.pallas_call(
            functools.partial(term_kernel, chips),
            out_shape=[
                jax.ShapeDtypeStruct((count, width // dp_count, WIDTH), BF16)
                for count in (chips, chips - 1)
            ]
            + [jax.ShapeDtypeStruct((width // dp_count, WIDTH), BF16)],
            in_specs=[smem] + [vmem] * (len(ready) + 1),
            out_specs=[vmem] * 3,
            compiler_params=params,
            cost_estimate=pl.CostEstimate(
                flops=2 * tokens * width * WIDTH,
                bytes_accessed=2 * width * WIDTH,
                transcendentals=0,
            ),
            name="term",
        )(jnp.stack([dp_idx, dp_idx]), *ready, mixed_above)
        grad_sum, incoming = sum_rows(
            mine, others, others_far, dp_count, incoming
        )
    else:
        grad_sum = lax.psum_scatter(
            dot_tn(jnp.concatenate(ready, axis=0), mixed_above), "dp", scatter_dimension=0, tiled=True
        )
    (carried,) = stage(sections - 1, incoming, previous)
    grad_sum = lax.ppermute(
        grad_sum.astype(BF16), "section", [(s, (s - 1) % sections) for s in range(sections)]
    )
    grad_sum = grad_sum.astype(F32) * float(tokens * dp_count) ** (-0.5)
    return carried.reshape(1, seqs, length, width), grad_sum[None]


def solution(mesh):
    in_specs = (
        P("section", "dp", None, None),
        P("dp", None),
        P("section", "dp", None),
        P("section", "dp", None),
        P("dp", None, None),
    )
    out_specs = (P("section", "dp", None, None), P("section", "dp", None))
    return jax.shard_map(
        per_device, mesh=mesh, in_specs=in_specs, out_specs=out_specs, check_vma=False
    )
```

```python
import functools
import math

import jax
import jax.numpy as jnp
from jax import lax
from jax.experimental import pallas as pl
from jax.experimental.pallas import tpu as pltpu
from jax.sharding import PartitionSpec as P

HEADS = 8
HD = 128
GRID = 32
WIDTH = HEADS * HD
SCALE = HD**-0.5
F32 = jnp.float32
BF16 = jnp.bfloat16
VMEM_LIMIT = 28 * 1024 * 1024


def ring_pairs(chips, step):
    order = [2 * r if r < chips // 2 else 2 * (chips - 1 - r) + 1 for r in range(chips)]
    return [
        (2 * order[r] + core, 2 * order[(r + step) % chips] + core)
        for r in range(chips)
        for core in range(2)
    ]


def chip_at(me, offset, chips):
    chip = me // 2
    place = jnp.where(chip % 2 == 0, chip // 2, chips - 1 - chip // 2)
    there = (place + (offset + chips)) % chips
    return jnp.where(there < chips // 2, 2 * there, 2 * (chips - 1 - there) + 1)


def swap_cores(value, dp_count):
    return lax.ppermute(value, "dp", [(i, i ^ 1) for i in range(dp_count)])


def in_hbm(value):
    return pltpu.with_memory_space_constraint(value, pltpu.HBM)


def gather_rows(shard, dp_count):
    chips = dp_count // 2
    far = chips // 2
    half = shard.shape[0] // 2
    ahead, behind = ring_pairs(chips, 1), ring_pairs(chips, -1)
    up = down = shard
    pieces = [(shard, 0, 0, 0)]
    for hop in range(1, far):
        up = lax.ppermute(up, "dp", ahead)
        down = lax.ppermute(down, "dp", behind)
        pieces += [(up, -hop, 0, 0), (down, hop, 0, 0)]
    up = lax.ppermute(up[:half], "dp", ahead)
    down = lax.ppermute(down[half:], "dp", behind)
    pieces += [(up, -far, 0, 0), (down, far, 0, half)]
    pieces = [(in_hbm(value), *place) for value, *place in pieces]
    pieces += [
        (in_hbm(swap_cores(value, dp_count)), offset, 1, row) for value, offset, _, row in pieces
    ]
    return [piece[0] for piece in pieces], [piece[1:] for piece in pieces]


def start_rows(pieces, places, chips, me, columns, target, sems):
    copies = []
    per_owner = target.shape[0] // (2 * chips)
    for number, (piece, place) in enumerate(zip(pieces, places)):
        rows = piece.shape[0]
        into = target
        if place is not None:
            offset, other, low = place
            owner = 2 * chip_at(me, offset, chips) + lax.rem(me + other, 2)
            into = target.at[pl.ds(pl.multiple_of(owner * per_owner + low, rows), rows)]
        copy = pltpu.make_async_copy(piece.at[:, columns], into, sems.at[number])
        copy.start()
        copies.append(copy)
    return copies


def head_spots(seqs, length):
    return [
        (slice(seq * length, seq * length + length), slice(head * HD, head * HD + HD))
        for head in range(HEADS)
        for seq in range(seqs)
    ]


def turn(value, cosine, sine):
    return value * cosine + pltpu.roll(value, HD // 2, 1) * sine


def rms_of(inputs_f):
    return lax.rsqrt(jnp.mean(inputs_f * inputs_f, axis=-1, keepdims=True) + 1e-06)


def dot_nt(a, b):
    return lax.dot_general(a, b, (((1,), (1,)), ((), ())), preferred_element_type=F32)


def dot_tn(a, b):
    return lax.dot_general(a, b, (((0,), (0,)), ((), ())), preferred_element_type=F32)


def rotation_tables(patch_index):
    length = patch_index.shape[1]
    lanes = lax.broadcasted_iota(jnp.int32, (length, HD), 1)
    slot = jnp.where(lanes < HD // 2, lanes, lanes - HD // 2)
    per_axis = (HD // 2 + 2) // 3
    spread = jnp.broadcast_to(patch_index.astype(F32), (HD, length))
    index = jnp.transpose(spread).astype(jnp.int32)
    place = jnp.where(
        slot % 3 == 0,
        index // (GRID * GRID),
        jnp.where(slot % 3 == 1, index // GRID % GRID, index % GRID),
    )
    rates = jnp.exp((slot // 3).astype(F32) * (-math.log(10000.0) / per_axis))
    angles = place.astype(F32) * rates
    sine = jnp.sin(angles)
    return jnp.cos(angles), jnp.where(lanes < HD // 2, -sine, sine)


def forward_kernel(places, chips, seqs, length, facts, x, patch_index, *rest):
    count = len(places)
    cosine, sine, queries, key_rows, values, probs, mixed, weights, normed, sems = rest[count:]
    copies = start_rows(
        rest[:count], places, chips, facts[0], pl.ds(0, 3 * WIDTH), weights, sems
    )
    x_f = x[...].astype(F32)
    normed[...] = (x_f * rms_of(x_f)).astype(BF16)
    for seq in range(seqs):
        rows = slice(seq * length, seq * length + length)
        cosine[rows], sine[rows] = rotation_tables(patch_index[seq : seq + 1])
    for copy in copies:
        copy.wait()
    for part, target in enumerate((queries, key_rows, values)):
        for column in range(0, WIDTH, 2 * HD):
            low = part * WIDTH + column
            block = jnp.dot(
                normed[...], weights[:, low : low + 2 * HD], preferred_element_type=F32
            )
            for head in range(2):
                one = block[:, head * HD : head * HD + HD]
                if part < 2:
                    one = turn(one, cosine[...], sine[...])
                target[:, column + head * HD : column + head * HD + HD] = one.astype(BF16)
    spots = head_spots(seqs, length)
    scores = [dot_nt(queries[spot], key_rows[spot]) * SCALE for spot in spots]
    highest = [jnp.max(one, axis=-1, keepdims=True) for one in scores]
    raised = [jnp.exp(one - top) for one, top in zip(scores, highest)]
    totals = [jnp.sum(one, axis=-1, keepdims=True) for one in raised]
    each = [one * (1.0 / total) for one, total in zip(raised, totals)]
    for number, prob in enumerate(each):
        probs[number] = prob
    for spot, prob in zip(spots, each):
        mixed[spot] = jnp.dot(
            prob.astype(BF16), values[spot], preferred_element_type=F32
        ).astype(BF16)


def heads_back_kernel(
    places, chips, seqs, length,
    facts, incoming, cosine, sine, queries, key_rows, values, probs, *rest,
):
    count = len(places)
    pieces = rest[:count]
    grad_proj, weights, grad_mixed, keys_here, values_here, sems, more_sems = rest[count:]

    @pl.when(facts[1] != 0)
    def _():
        copies = start_rows(
            pieces, places, chips, facts[0], pl.ds(3 * WIDTH, WIDTH), weights, sems
        )
        more = [
            pltpu.make_async_copy(key_rows, keys_here, more_sems.at[0]),
            pltpu.make_async_copy(values, values_here, more_sems.at[1]),
        ]
        for copy in more:
            copy.start()
        for copy in copies:
            copy.wait()
        for column in range(0, WIDTH, 2 * HD):
            grad_mixed[:, column : column + 2 * HD] = jnp.dot(
                incoming[...], weights[:, column : column + 2 * HD], preferred_element_type=F32
            ).astype(BF16)
        for copy in more:
            copy.wait()
        spots = head_spots(seqs, length)
        each = [probs[number] for number in range(len(spots))]
        grad_probs = [dot_nt(grad_mixed[spot], values_here[spot]) for spot in spots]
        grad_values = [
            dot_tn(prob.astype(BF16), grad_mixed[spot]) for prob, spot in zip(each, spots)
        ]
        shifts = [
            jnp.sum(grad * prob, axis=-1, keepdims=True) for grad, prob in zip(grad_probs, each)
        ]
        grad_scores = [
            (prob * (grad - shift) * SCALE).astype(BF16)
            for prob, grad, shift in zip(each, grad_probs, shifts)
        ]
        grad_q = [
            jnp.dot(grad, keys_here[spot], preferred_element_type=F32)
            for grad, spot in zip(grad_scores, spots)
        ]
        grad_k = [dot_tn(grad, queries[spot]) for grad, spot in zip(grad_scores, spots)]
        for (rows, columns), one_q, one_k, one_v in zip(spots, grad_q, grad_k, grad_values):
            low = columns.start
            back = -sine[rows]
            grad_proj[rows, low : low + HD] = turn(one_q, cosine[rows], back).astype(BF16)
            low += WIDTH
            grad_proj[rows, low : low + HD] = turn(one_k, cosine[rows], back).astype(BF16)
            low += WIDTH
            grad_proj[rows, low : low + HD] = one_v.astype(BF16)


def inputs_back_kernel(places, chips, facts, incoming, previous, x, grad_proj, *rest):
    count = len(places)
    pieces = rest[:count]
    grad_inputs, weights, grad_normed, sems = rest[count:]

    @pl.when(facts[1] != 0)
    def _():
        copies = start_rows(pieces, places, chips, facts[0], pl.ds(0, 3 * WIDTH), weights, sems)
        x_f = x[...].astype(F32)
        inv_rms = rms_of(x_f)
        for copy in copies:
            copy.wait()
        for low in range(0, x.shape[1], 256):
            grad_normed[:, low : low + 256] = dot_nt(grad_proj[...], weights[low : low + 256, :])
        g_normed = grad_normed[...]
        shift = jnp.mean(g_normed * x_f, axis=-1, keepdims=True)
        grad_inputs[...] = (
            incoming[...].astype(F32) + inv_rms * g_normed - x_f * (inv_rms**3 * shift)
        ).astype(BF16)

    @pl.when(facts[1] == 0)
    def _():
        grad_inputs[...] = previous[...]


def far_offsets(chips):
    first = [chips // 2 - 1, chips // 2 + 1]
    return first, [offset for offset in range(chips) if offset not in first]


def term_kernel(chips, facts, incoming, mixed, mine, others_first, others):
    me = facts[0]
    rows = incoming.shape[1] // (2 * chips)
    upper = lax.rem(me, 2) == 0
    for offsets, target in zip(far_offsets(chips), (others_first, others)):
        for number, offset in enumerate(offsets):
            chip = chip_at(me, offset, chips)
            column = pl.multiple_of(chip * 2 * rows, 2 * rows)
            term = dot_tn(incoming[:, pl.ds(column, 2 * rows)], mixed[...])
            first, second = term[:rows], term[rows:]
            mine[offset] = jnp.where(upper, first, second).astype(BF16)
            target[number] = jnp.where(upper, second, first).astype(BF16)


def sum_rows(mine, others_first, others, dp_count, tied):
    chips = dp_count // 2
    far = chips // 2
    ahead, behind = ring_pairs(chips, 1), ring_pairs(chips, -1)
    from_core = {}
    for offsets, terms in zip(far_offsets(chips), (others_first, others)):
        arrived = swap_cores(terms, dp_count)
        from_core.update((offset, arrived[number]) for number, offset in enumerate(offsets))

    def held(offset):
        return mine[offset].astype(F32) + from_core[offset].astype(F32)

    up = lax.ppermute(held(far - 1).astype(BF16), "dp", ahead)
    down = lax.ppermute(held(far + 1).astype(BF16), "dp", behind)
    straight, up = lax.optimization_barrier((held(far).astype(BF16), up))
    across = lax.ppermute(straight, "dp", ring_pairs(chips, far))
    for hop in range(far - 2, 0, -1):
        if hop == 1:
            up, down, across, tied = lax.optimization_barrier((up, down, across, tied))
        else:
            up, down = lax.optimization_barrier((up, down))
        up = lax.ppermute((held(hop) + up.astype(F32)).astype(BF16), "dp", ahead)
        down = lax.ppermute((held(chips - hop) + down.astype(F32)).astype(BF16), "dp", behind)
    return held(0) + across.astype(F32) + up.astype(F32) + down.astype(F32), tied


def per_device(section_inputs, patch_index, w_qkv, w_out, out_cotangent):
    seqs, length, width = section_inputs.shape[1:]
    tokens = seqs * length
    sections = lax.axis_size("section")
    dp_count = lax.axis_size("dp")
    chips = dp_count // 2
    by_ring = dp_count % 4 == 0 and 4 <= chips <= 8
    dp_idx = lax.axis_index("dp").astype(jnp.int32)
    section_idx = lax.axis_index("section")
    x = section_inputs[0].reshape(tokens, width)
    shard = jnp.concatenate([w_qkv[0], w_out[0]], axis=1)
    if by_ring:
        pieces, places = gather_rows(shard, dp_count)
    else:
        pieces, places = [lax.all_gather(shard, "dp", axis=0, tiled=True)], [None]

    smem = pl.BlockSpec(memory_space=pltpu.SMEM)
    vmem = pl.BlockSpec(memory_space=pltpu.VMEM)
    anywhere = pl.BlockSpec(memory_space=pltpu.HBM)
    params = pltpu.CompilerParams(vmem_limit_bytes=VMEM_LIMIT)
    like = jax.ShapeDtypeStruct((tokens, width), BF16)
    heads_like = jax.ShapeDtypeStruct((tokens, WIDTH), BF16)

    table_like = jax.ShapeDtypeStruct((tokens, HD), F32)
    cosine, sine, queries, key_rows, values, probs, mixed = pl.pallas_call(
        functools.partial(forward_kernel, places, chips, seqs, length),
        out_shape=[table_like] * 2
        + [heads_like, pltpu.HBM((tokens, WIDTH), BF16), pltpu.HBM((tokens, WIDTH), BF16)]
        + [jax.ShapeDtypeStruct((HEADS * seqs, length, length), F32), heads_like],
        in_specs=[smem, vmem, vmem] + [anywhere] * len(pieces),
        out_specs=[vmem] * 7,
        scratch_shapes=[
            pltpu.VMEM((width, 3 * WIDTH), BF16),
            pltpu.VMEM((tokens, width), BF16),
            pltpu.SemaphoreType.DMA((len(pieces),)),
        ],
        compiler_params=params,
        cost_estimate=pl.CostEstimate(
            flops=2 * tokens * width * 3 * WIDTH,
            bytes_accessed=6 * width * WIDTH,
            transcendentals=0,
        ),
        name="forward",
    )(jnp.stack([dp_idx, dp_idx]), x, patch_index, *pieces)
    key_rows, values = in_hbm(key_rows), in_hbm(values)
    mixed_above = lax.ppermute(mixed, "section", [(s, (s + 1) % sections) for s in range(sections)])

    def stage(number, incoming, previous):
        active = (section_idx == sections - 1 - number).astype(jnp.int32)
        facts = jnp.stack([dp_idx, active])
        grad_proj = pl.pallas_call(
            functools.partial(heads_back_kernel, places, chips, seqs, length),
            out_shape=jax.ShapeDtypeStruct((tokens, 3 * WIDTH), BF16),
            in_specs=[smem] + [vmem] * 4 + [anywhere] * 2 + [vmem] + [anywhere] * len(pieces),
            out_specs=vmem,
            scratch_shapes=[
                pltpu.VMEM((width, WIDTH), BF16),
                pltpu.VMEM((tokens, WIDTH), BF16),
                pltpu.VMEM((tokens, WIDTH), BF16),
                pltpu.VMEM((tokens, WIDTH), BF16),
                pltpu.SemaphoreType.DMA((len(pieces),)),
                pltpu.SemaphoreType.DMA((2,)),
            ],
            compiler_params=params,
            cost_estimate=pl.CostEstimate(
                flops=2 * tokens * width * WIDTH,
                bytes_accessed=8 * width * WIDTH,
                transcendentals=0,
            ),
            name="heads_back",
        )(facts, incoming, cosine, sine, queries, key_rows, values, probs, *pieces)
        return pl.pallas_call(
            functools.partial(inputs_back_kernel, places, chips),
            out_shape=like,
            in_specs=[smem] + [vmem] * 4 + [anywhere] * len(pieces),
            out_specs=vmem,
            scratch_shapes=[
                pltpu.VMEM((width, 3 * WIDTH), BF16),
                pltpu.VMEM((tokens, width), F32),
                pltpu.SemaphoreType.DMA((len(pieces),)),
            ],
            compiler_params=params,
            cost_estimate=pl.CostEstimate(
                flops=2 * tokens * width * 3 * WIDTH,
                bytes_accessed=8 * width * WIDTH,
                transcendentals=0,
            ),
            name="inputs_back",
        )(facts, incoming, previous, x, grad_proj, *pieces)

    incoming = carried = out_cotangent.reshape(tokens, width)
    back = [(s, s - 1) for s in range(1, sections)]
    for number in range(sections - 1):
        carried = stage(number, incoming, carried)
        incoming = lax.ppermute(carried, "section", back)
    ready = carried

    if by_ring:
        first, rest = far_offsets(chips)
        mine, others_first, others = pl.pallas_call(
            functools.partial(term_kernel, chips),
            out_shape=[
                jax.ShapeDtypeStruct((count, width // dp_count, WIDTH), BF16)
                for count in (chips, len(first), len(rest))
            ],
            in_specs=[smem, vmem, vmem],
            out_specs=[vmem] * 3,
            compiler_params=params,
            cost_estimate=pl.CostEstimate(
                flops=2 * tokens * width * WIDTH,
                bytes_accessed=2 * width * WIDTH,
                transcendentals=0,
            ),
            name="term",
        )(jnp.stack([dp_idx, dp_idx]), ready, mixed_above)
        grad_sum, incoming = sum_rows(
            mine, others_first, others, dp_count, incoming
        )
    else:
        grad_sum = lax.psum_scatter(
            dot_tn(ready, mixed_above), "dp", scatter_dimension=0, tiled=True
        )
    carried = stage(sections - 1, incoming, carried)
    grad_sum = lax.ppermute(
        grad_sum.astype(BF16), "section", [(s, (s - 1) % sections) for s in range(sections)]
    )
    grad_sum = grad_sum.astype(F32) * float(tokens * dp_count) ** (-0.5)
    return carried.reshape(1, seqs, length, width), grad_sum[None]


def solution(mesh):
    in_specs = (
        P("section", "dp", None, None),
        P("dp", None),
        P("section", "dp", None),
        P("section", "dp", None),
        P("dp", None, None),
    )
    out_specs = (P("section", "dp", None, None), P("section", "dp", None))
    return jax.shard_map(
        per_device, mesh=mesh, in_specs=in_specs, out_specs=out_specs, check_vma=False
    )
```

```python
import functools
import math

import jax
import jax.numpy as jnp
from jax import lax
from jax.experimental import pallas as pl
from jax.experimental.pallas import tpu as pltpu
from jax.sharding import PartitionSpec as P

HEADS = 8
HD = 128
GRID = 32
WIDTH = HEADS * HD
SCALE = HD**-0.5
F32 = jnp.float32
BF16 = jnp.bfloat16
VMEM_LIMIT = 28 * 1024 * 1024


def ring_pairs(chips, step):
    order = [2 * r if r < chips // 2 else 2 * (chips - 1 - r) + 1 for r in range(chips)]
    return [
        (2 * order[r] + core, 2 * order[(r + step) % chips] + core)
        for r in range(chips)
        for core in range(2)
    ]


def chip_at(me, offset, chips):
    chip = me // 2
    place = jnp.where(chip % 2 == 0, chip // 2, chips - 1 - chip // 2)
    there = (place + (offset + chips)) % chips
    return jnp.where(there < chips // 2, 2 * there, 2 * (chips - 1 - there) + 1)


def swap_cores(value, dp_count):
    return lax.ppermute(value, "dp", [(i, i ^ 1) for i in range(dp_count)])


def in_hbm(value):
    return pltpu.with_memory_space_constraint(value, pltpu.HBM)


def gather_rows(shard, dp_count):
    chips = dp_count // 2
    far = chips // 2
    half = shard.shape[0] // 2
    ahead, behind = ring_pairs(chips, 1), ring_pairs(chips, -1)
    up = down = shard
    pieces = [(shard, 0, 0, 0)]
    for hop in range(1, far):
        up = lax.ppermute(up, "dp", ahead)
        down = lax.ppermute(down, "dp", behind)
        pieces += [(up, -hop, 0, 0), (down, hop, 0, 0)]
    up = lax.ppermute(up[:half], "dp", ahead)
    down = lax.ppermute(down[half:], "dp", behind)
    pieces += [(up, -far, 0, 0), (down, far, 0, half)]
    pieces = [(in_hbm(value), *place) for value, *place in pieces]
    pieces += [
        (in_hbm(swap_cores(value, dp_count)), offset, 1, row) for value, offset, _, row in pieces
    ]
    return [piece[0] for piece in pieces], [piece[1:] for piece in pieces]


def start_rows(pieces, places, chips, me, columns, target, sem_at):
    copies = []
    per_owner = target.shape[0] // (2 * chips)
    for number, (piece, place) in enumerate(zip(pieces, places)):
        rows = piece.shape[0]
        into = target
        if place is not None:
            offset, other, low = place
            owner = 2 * chip_at(me, offset, chips) + lax.rem(me + other, 2)
            into = target.at[pl.ds(pl.multiple_of(owner * per_owner + low, rows), rows)]
        copy = pltpu.make_async_copy(piece.at[:, columns], into, sem_at(number))
        copy.start()
        copies.append(copy)
    return copies


def start_parts(pieces, places, chips, me, target, sems):
    return [
        start_rows(
            pieces, places, chips, me, pl.ds(part * WIDTH, WIDTH), target.at[part],
            lambda number, part=part: sems.at[part, number],
        )
        for part in range(3)
    ]


def head_spots(seqs, length):
    return [
        (slice(seq * length, seq * length + length), slice(head * HD, head * HD + HD))
        for head in range(HEADS)
        for seq in range(seqs)
    ]


def turn(value, cosine, sine):
    return value * cosine + pltpu.roll(value, HD // 2, 1) * sine


def rms_of(inputs_f):
    return lax.rsqrt(jnp.mean(inputs_f * inputs_f, axis=-1, keepdims=True) + 1e-06)


def dot_nt(a, b):
    return lax.dot_general(a, b, (((1,), (1,)), ((), ())), preferred_element_type=F32)


def dot_tn(a, b):
    return lax.dot_general(a, b, (((0,), (0,)), ((), ())), preferred_element_type=F32)


def rotation_tables(patch_index):
    length = patch_index.shape[1]
    lanes = lax.broadcasted_iota(jnp.int32, (length, HD), 1)
    slot = jnp.where(lanes < HD // 2, lanes, lanes - HD // 2)
    per_axis = (HD // 2 + 2) // 3
    spread = jnp.broadcast_to(patch_index.astype(F32), (HD, length))
    index = jnp.transpose(spread).astype(jnp.int32)
    place = jnp.where(
        slot % 3 == 0,
        index // (GRID * GRID),
        jnp.where(slot % 3 == 1, index // GRID % GRID, index % GRID),
    )
    rates = jnp.exp((slot // 3).astype(F32) * (-math.log(10000.0) / per_axis))
    angles = place.astype(F32) * rates
    sine = jnp.sin(angles)
    return jnp.cos(angles), jnp.where(lanes < HD // 2, -sine, sine)


def forward_kernel(places, chips, seqs, length, facts, x, patch_index, *rest):
    count = len(places)
    cosine, sine, queries, key_rows, values, probs, mixed, weights, normed, sems = rest[count:]
    copies = start_parts(rest[:count], places, chips, facts[0], weights, sems)
    x_f = x[...].astype(F32)
    normed[...] = (x_f * rms_of(x_f)).astype(BF16)
    for seq in range(seqs):
        rows = slice(seq * length, seq * length + length)
        cosine[rows], sine[rows] = rotation_tables(patch_index[seq : seq + 1])
    for part, target in enumerate((queries, key_rows, values)):
        for copy in copies[part]:
            copy.wait()
        for column in range(0, WIDTH, 2 * HD):
            block = jnp.dot(
                normed[...],
                weights[part, :, column : column + 2 * HD],
                preferred_element_type=F32,
            )
            for head in range(2):
                one = block[:, head * HD : head * HD + HD]
                if part < 2:
                    one = turn(one, cosine[...], sine[...])
                target[:, column + head * HD : column + head * HD + HD] = one.astype(BF16)
    spots = head_spots(seqs, length)
    scores = [dot_nt(queries[spot], key_rows[spot]) * SCALE for spot in spots]
    highest = [jnp.max(one, axis=-1, keepdims=True) for one in scores]
    raised = [jnp.exp(one - top) for one, top in zip(scores, highest)]
    totals = [jnp.sum(one, axis=-1, keepdims=True) for one in raised]
    each = [one * (1.0 / total) for one, total in zip(raised, totals)]
    for number, prob in enumerate(each):
        probs[number] = prob
    for spot, prob in zip(spots, each):
        mixed[spot] = jnp.dot(
            prob.astype(BF16), values[spot], preferred_element_type=F32
        ).astype(BF16)


def heads_back_kernel(
    places, chips, seqs, length,
    facts, incoming, cosine, sine, queries, key_rows, values, probs, *rest,
):
    count = len(places)
    pieces = rest[:count]
    grad_proj, weights, grad_mixed, keys_here, values_here, sems, more_sems = rest[count:]

    @pl.when(facts[1] != 0)
    def _():
        copies = start_rows(
            pieces, places, chips, facts[0], pl.ds(3 * WIDTH, WIDTH), weights,
            lambda number: sems.at[number],
        )
        more = [
            pltpu.make_async_copy(key_rows, keys_here, more_sems.at[0]),
            pltpu.make_async_copy(values, values_here, more_sems.at[1]),
        ]
        for copy in more:
            copy.start()
        for copy in copies:
            copy.wait()
        for column in range(0, WIDTH, 2 * HD):
            grad_mixed[:, column : column + 2 * HD] = jnp.dot(
                incoming[...], weights[:, column : column + 2 * HD], preferred_element_type=F32
            ).astype(BF16)
        for copy in more:
            copy.wait()
        spots = head_spots(seqs, length)
        each = [probs[number] for number in range(len(spots))]
        grad_probs = [dot_nt(grad_mixed[spot], values_here[spot]) for spot in spots]
        grad_values = [
            dot_tn(prob.astype(BF16), grad_mixed[spot]) for prob, spot in zip(each, spots)
        ]
        shifts = [
            jnp.sum(grad * prob, axis=-1, keepdims=True) for grad, prob in zip(grad_probs, each)
        ]
        grad_scores = [
            (prob * (grad - shift) * SCALE).astype(BF16)
            for prob, grad, shift in zip(each, grad_probs, shifts)
        ]
        grad_q = [
            jnp.dot(grad, keys_here[spot], preferred_element_type=F32)
            for grad, spot in zip(grad_scores, spots)
        ]
        grad_k = [dot_tn(grad, queries[spot]) for grad, spot in zip(grad_scores, spots)]
        for (rows, columns), one_q, one_k, one_v in zip(spots, grad_q, grad_k, grad_values):
            low = columns.start
            back = -sine[rows]
            grad_proj[rows, low : low + HD] = turn(one_q, cosine[rows], back).astype(BF16)
            low += WIDTH
            grad_proj[rows, low : low + HD] = turn(one_k, cosine[rows], back).astype(BF16)
            low += WIDTH
            grad_proj[rows, low : low + HD] = one_v.astype(BF16)


def inputs_back_kernel(places, chips, facts, incoming, previous, x, grad_proj, *rest):
    count = len(places)
    pieces = rest[:count]
    grad_inputs, weights, grad_normed, sems = rest[count:]

    @pl.when(facts[1] != 0)
    def _():
        copies = start_parts(pieces, places, chips, facts[0], weights, sems)
        x_f = x[...].astype(F32)
        inv_rms = rms_of(x_f)
        for part in range(3):
            for copy in copies[part]:
                copy.wait()
            taken = grad_proj[:, part * WIDTH : part * WIDTH + WIDTH]
            for low in range(0, x.shape[1], 256):
                product = dot_nt(taken, weights[part, low : low + 256, :])
                if part:
                    product = grad_normed[:, low : low + 256] + product
                grad_normed[:, low : low + 256] = product
        g_normed = grad_normed[...]
        shift = jnp.mean(g_normed * x_f, axis=-1, keepdims=True)
        grad_inputs[...] = (
            incoming[...].astype(F32) + inv_rms * g_normed - x_f * (inv_rms**3 * shift)
        ).astype(BF16)

    @pl.when(facts[1] == 0)
    def _():
        grad_inputs[...] = previous[...]


def far_offsets(chips):
    first = [chips // 2 - 1, chips // 2 + 1]
    return first, [offset for offset in range(chips) if offset not in first]


def term_kernel(chips, facts, incoming, mixed, mine, others_first, others):
    me = facts[0]
    rows = incoming.shape[1] // (2 * chips)
    upper = lax.rem(me, 2) == 0
    for offsets, target in zip(far_offsets(chips), (others_first, others)):
        for number, offset in enumerate(offsets):
            chip = chip_at(me, offset, chips)
            column = pl.multiple_of(chip * 2 * rows, 2 * rows)
            term = dot_tn(incoming[:, pl.ds(column, 2 * rows)], mixed[...])
            first, second = term[:rows], term[rows:]
            mine[offset] = jnp.where(upper, first, second).astype(BF16)
            target[number] = jnp.where(upper, second, first).astype(BF16)


def sum_rows(mine, others_first, others, dp_count, tied):
    chips = dp_count // 2
    far = chips // 2
    ahead, behind = ring_pairs(chips, 1), ring_pairs(chips, -1)
    from_core = {}
    for offsets, terms in zip(far_offsets(chips), (others_first, others)):
        arrived = swap_cores(terms, dp_count)
        from_core.update((offset, arrived[number]) for number, offset in enumerate(offsets))

    def held(offset):
        return mine[offset].astype(F32) + from_core[offset].astype(F32)

    up = lax.ppermute(held(far - 1).astype(BF16), "dp", ahead)
    down = lax.ppermute(held(far + 1).astype(BF16), "dp", behind)
    straight, up = lax.optimization_barrier((held(far).astype(BF16), up))
    across = lax.ppermute(straight, "dp", ring_pairs(chips, far))
    for hop in range(far - 2, 0, -1):
        if hop == 1:
            up, down, across, tied = lax.optimization_barrier((up, down, across, tied))
        else:
            up, down = lax.optimization_barrier((up, down))
        up = lax.ppermute((held(hop) + up.astype(F32)).astype(BF16), "dp", ahead)
        down = lax.ppermute((held(chips - hop) + down.astype(F32)).astype(BF16), "dp", behind)
    return held(0) + across.astype(F32) + up.astype(F32) + down.astype(F32), tied


def per_device(section_inputs, patch_index, w_qkv, w_out, out_cotangent):
    seqs, length, width = section_inputs.shape[1:]
    tokens = seqs * length
    sections = lax.axis_size("section")
    dp_count = lax.axis_size("dp")
    chips = dp_count // 2
    by_ring = dp_count % 4 == 0 and 4 <= chips <= 8
    dp_idx = lax.axis_index("dp").astype(jnp.int32)
    section_idx = lax.axis_index("section")
    x = section_inputs[0].reshape(tokens, width)
    shard = jnp.concatenate([w_qkv[0], w_out[0]], axis=1)
    if by_ring:
        pieces, places = gather_rows(shard, dp_count)
    else:
        pieces, places = [lax.all_gather(shard, "dp", axis=0, tiled=True)], [None]

    smem = pl.BlockSpec(memory_space=pltpu.SMEM)
    vmem = pl.BlockSpec(memory_space=pltpu.VMEM)
    anywhere = pl.BlockSpec(memory_space=pltpu.HBM)
    params = pltpu.CompilerParams(vmem_limit_bytes=VMEM_LIMIT)
    like = jax.ShapeDtypeStruct((tokens, width), BF16)
    heads_like = jax.ShapeDtypeStruct((tokens, WIDTH), BF16)

    table_like = jax.ShapeDtypeStruct((tokens, HD), F32)
    cosine, sine, queries, key_rows, values, probs, mixed = pl.pallas_call(
        functools.partial(forward_kernel, places, chips, seqs, length),
        out_shape=[table_like] * 2
        + [heads_like, pltpu.HBM((tokens, WIDTH), BF16), pltpu.HBM((tokens, WIDTH), BF16)]
        + [jax.ShapeDtypeStruct((HEADS * seqs, length, length), F32), heads_like],
        in_specs=[smem, vmem, vmem] + [anywhere] * len(pieces),
        out_specs=[vmem] * 7,
        scratch_shapes=[
            pltpu.VMEM((3, width, WIDTH), BF16),
            pltpu.VMEM((tokens, width), BF16),
            pltpu.SemaphoreType.DMA((3, len(pieces))),
        ],
        compiler_params=params,
        cost_estimate=pl.CostEstimate(
            flops=2 * tokens * width * 3 * WIDTH,
            bytes_accessed=6 * width * WIDTH,
            transcendentals=0,
        ),
        name="forward",
    )(jnp.stack([dp_idx, dp_idx]), x, patch_index, *pieces)
    key_rows, values = in_hbm(key_rows), in_hbm(values)
    mixed_above = lax.ppermute(mixed, "section", [(s, (s + 1) % sections) for s in range(sections)])

    def stage(number, incoming, previous):
        active = (section_idx == sections - 1 - number).astype(jnp.int32)
        facts = jnp.stack([dp_idx, active])
        grad_proj = pl.pallas_call(
            functools.partial(heads_back_kernel, places, chips, seqs, length),
            out_shape=jax.ShapeDtypeStruct((tokens, 3 * WIDTH), BF16),
            in_specs=[smem] + [vmem] * 4 + [anywhere] * 2 + [vmem] + [anywhere] * len(pieces),
            out_specs=vmem,
            scratch_shapes=[
                pltpu.VMEM((width, WIDTH), BF16),
                pltpu.VMEM((tokens, WIDTH), BF16),
                pltpu.VMEM((tokens, WIDTH), BF16),
                pltpu.VMEM((tokens, WIDTH), BF16),
                pltpu.SemaphoreType.DMA((len(pieces),)),
                pltpu.SemaphoreType.DMA((2,)),
            ],
            compiler_params=params,
            cost_estimate=pl.CostEstimate(
                flops=2 * tokens * width * WIDTH,
                bytes_accessed=8 * width * WIDTH,
                transcendentals=0,
            ),
            name="heads_back",
        )(facts, incoming, cosine, sine, queries, key_rows, values, probs, *pieces)
        return pl.pallas_call(
            functools.partial(inputs_back_kernel, places, chips),
            out_shape=like,
            in_specs=[smem] + [vmem] * 4 + [anywhere] * len(pieces),
            out_specs=vmem,
            scratch_shapes=[
                pltpu.VMEM((3, width, WIDTH), BF16),
                pltpu.VMEM((tokens, width), F32),
                pltpu.SemaphoreType.DMA((3, len(pieces))),
            ],
            compiler_params=params,
            cost_estimate=pl.CostEstimate(
                flops=2 * tokens * width * 3 * WIDTH,
                bytes_accessed=8 * width * WIDTH,
                transcendentals=0,
            ),
            name="inputs_back",
        )(facts, incoming, previous, x, grad_proj, *pieces)

    incoming = carried = out_cotangent.reshape(tokens, width)
    back = [(s, s - 1) for s in range(1, sections)]
    for number in range(sections - 1):
        carried = stage(number, incoming, carried)
        incoming = lax.ppermute(carried, "section", back)
    ready = carried

    if by_ring:
        first, rest = far_offsets(chips)
        mine, others_first, others = pl.pallas_call(
            functools.partial(term_kernel, chips),
            out_shape=[
                jax.ShapeDtypeStruct((count, width // dp_count, WIDTH), BF16)
                for count in (chips, len(first), len(rest))
            ],
            in_specs=[smem, vmem, vmem],
            out_specs=[vmem] * 3,
            compiler_params=params,
            cost_estimate=pl.CostEstimate(
                flops=2 * tokens * width * WIDTH,
                bytes_accessed=2 * width * WIDTH,
                transcendentals=0,
            ),
            name="term",
        )(jnp.stack([dp_idx, dp_idx]), ready, mixed_above)
        grad_sum, incoming = sum_rows(
            mine, others_first, others, dp_count, incoming
        )
    else:
        grad_sum = lax.psum_scatter(
            dot_tn(ready, mixed_above), "dp", scatter_dimension=0, tiled=True
        )
    carried = stage(sections - 1, incoming, carried)
    grad_sum = lax.ppermute(
        grad_sum.astype(BF16), "section", [(s, (s - 1) % sections) for s in range(sections)]
    )
    grad_sum = grad_sum.astype(F32) * float(tokens * dp_count) ** (-0.5)
    return carried.reshape(1, seqs, length, width), grad_sum[None]


def solution(mesh):
    in_specs = (
        P("section", "dp", None, None),
        P("dp", None),
        P("section", "dp", None),
        P("section", "dp", None),
        P("dp", None, None),
    )
    out_specs = (P("section", "dp", None, None), P("section", "dp", None))
    return jax.shard_map(
        per_device, mesh=mesh, in_specs=in_specs, out_specs=out_specs, check_vma=False
    )
```

```python
import functools
import math

import jax
import jax.numpy as jnp
from jax import lax
from jax.experimental import pallas as pl
from jax.experimental.pallas import tpu as pltpu
from jax.sharding import PartitionSpec as P

HEADS = 8
HD = 128
GRID = 32
WIDTH = HEADS * HD
SCALE = HD**-0.5
F32 = jnp.float32
BF16 = jnp.bfloat16
VMEM_LIMIT = 28 * 1024 * 1024


def ring_pairs(chips, step):
    order = [2 * r if r < chips // 2 else 2 * (chips - 1 - r) + 1 for r in range(chips)]
    return [
        (2 * order[r] + core, 2 * order[(r + step) % chips] + core)
        for r in range(chips)
        for core in range(2)
    ]


def chip_at(me, offset, chips):
    chip = me // 2
    place = jnp.where(chip % 2 == 0, chip // 2, chips - 1 - chip // 2)
    there = (place + (offset + chips)) % chips
    return jnp.where(there < chips // 2, 2 * there, 2 * (chips - 1 - there) + 1)


def swap_cores(value, dp_count):
    return lax.ppermute(value, "dp", [(i, i ^ 1) for i in range(dp_count)])


def in_hbm(value):
    return pltpu.with_memory_space_constraint(value, pltpu.HBM)


def gather_rows(shard, dp_count):
    chips = dp_count // 2
    far = chips // 2
    half = shard.shape[0] // 2
    ahead, behind = ring_pairs(chips, 1), ring_pairs(chips, -1)
    up = down = shard
    pieces = [(shard, 0, 0, 0)]
    for hop in range(1, far):
        up = lax.ppermute(up, "dp", ahead)
        down = lax.ppermute(down, "dp", behind)
        pieces += [(up, -hop, 0, 0), (down, hop, 0, 0)]
    up = lax.ppermute(up[:half], "dp", ahead)
    down = lax.ppermute(down[half:], "dp", behind)
    pieces += [(up, -far, 0, 0), (down, far, 0, half)]
    pieces = [(in_hbm(value), *place) for value, *place in pieces]
    pieces += [
        (in_hbm(swap_cores(value, dp_count)), offset, 1, row) for value, offset, _, row in pieces
    ]
    return [piece[0] for piece in pieces], [piece[1:] for piece in pieces]


def start_rows(pieces, places, chips, me, columns, target, sem_at):
    copies = []
    per_owner = target.shape[0] // (2 * chips)
    for number, (piece, place) in enumerate(zip(pieces, places)):
        rows = piece.shape[0]
        into = target
        if place is not None:
            offset, other, low = place
            owner = 2 * chip_at(me, offset, chips) + lax.rem(me + other, 2)
            into = target.at[pl.ds(pl.multiple_of(owner * per_owner + low, rows), rows)]
        copy = pltpu.make_async_copy(piece.at[:, columns], into, sem_at(number))
        copy.start()
        copies.append(copy)
    return copies


def start_parts(pieces, places, chips, me, target, sems):
    return [
        start_rows(
            pieces, places, chips, me, pl.ds(part * WIDTH, WIDTH), target.at[part],
            lambda number, part=part: sems.at[part, number],
        )
        for part in range(3)
    ]


def head_spots(seqs, length):
    return [
        (slice(seq * length, seq * length + length), slice(head * HD, head * HD + HD))
        for head in range(HEADS)
        for seq in range(seqs)
    ]


def turn(value, cosine, sine):
    return value * cosine + pltpu.roll(value, HD // 2, 1) * sine


def rms_of(inputs_f):
    return lax.rsqrt(jnp.mean(inputs_f * inputs_f, axis=-1, keepdims=True) + 1e-06)


def dot_nt(a, b):
    return lax.dot_general(a, b, (((1,), (1,)), ((), ())), preferred_element_type=F32)


def dot_tn(a, b):
    return lax.dot_general(a, b, (((0,), (0,)), ((), ())), preferred_element_type=F32)


def rotation_tables(patch_index):
    length = patch_index.shape[1]
    lanes = lax.broadcasted_iota(jnp.int32, (length, HD), 1)
    slot = jnp.where(lanes < HD // 2, lanes, lanes - HD // 2)
    per_axis = (HD // 2 + 2) // 3
    spread = jnp.broadcast_to(patch_index.astype(F32), (HD, length))
    index = jnp.transpose(spread).astype(jnp.int32)
    place = jnp.where(
        slot % 3 == 0,
        index // (GRID * GRID),
        jnp.where(slot % 3 == 1, index // GRID % GRID, index % GRID),
    )
    rates = jnp.exp((slot // 3).astype(F32) * (-math.log(10000.0) / per_axis))
    angles = place.astype(F32) * rates
    sine = jnp.sin(angles)
    return jnp.cos(angles), jnp.where(lanes < HD // 2, -sine, sine)


def forward_kernel(places, chips, seqs, length, facts, x, patch_index, *rest):
    count = len(places)
    cosine, sine, queries, key_rows, values, probs, mixed, weights, normed, sems = rest[count:]
    copies = start_parts(rest[:count], places, chips, facts[0], weights, sems)
    x_f = x[...].astype(F32)
    normed[...] = (x_f * rms_of(x_f)).astype(BF16)
    for seq in range(seqs):
        rows = slice(seq * length, seq * length + length)
        cosine[rows], sine[rows] = rotation_tables(patch_index[seq : seq + 1])
    for part, target in enumerate((queries, key_rows, values)):
        for copy in copies[part]:
            copy.wait()
        for column in range(0, WIDTH, 2 * HD):
            block = jnp.dot(
                normed[...],
                weights[part, :, column : column + 2 * HD],
                preferred_element_type=F32,
            )
            for head in range(2):
                one = block[:, head * HD : head * HD + HD]
                if part < 2:
                    one = turn(one, cosine[...], sine[...])
                target[:, column + head * HD : column + head * HD + HD] = one.astype(BF16)
    spots = head_spots(seqs, length)
    scores = [dot_nt(queries[spot], key_rows[spot]) * SCALE for spot in spots]
    highest = [jnp.max(one, axis=-1, keepdims=True) for one in scores]
    raised = [jnp.exp(one - top) for one, top in zip(scores, highest)]
    totals = [jnp.sum(one, axis=-1, keepdims=True) for one in raised]
    each = [one * (1.0 / total) for one, total in zip(raised, totals)]
    for number, prob in enumerate(each):
        probs[number] = prob
    for spot, prob in zip(spots, each):
        mixed[spot] = jnp.dot(
            prob.astype(BF16), values[spot], preferred_element_type=F32
        ).astype(BF16)


def heads_back_kernel(
    places, chips, seqs, length,
    facts, incoming, cosine, sine, queries, key_rows, values, probs, *rest,
):
    count = len(places)
    pieces = rest[:count]
    grad_proj, weights, grad_mixed, keys_here, values_here, sems, more_sems = rest[count:]

    @pl.when(facts[1] != 0)
    def _():
        copies = start_rows(
            pieces, places, chips, facts[0], pl.ds(3 * WIDTH, WIDTH), weights,
            lambda number: sems.at[number],
        )
        more = [
            pltpu.make_async_copy(key_rows, keys_here, more_sems.at[0]),
            pltpu.make_async_copy(values, values_here, more_sems.at[1]),
        ]
        for copy in more:
            copy.start()
        for copy in copies:
            copy.wait()
        for column in range(0, WIDTH, 2 * HD):
            grad_mixed[:, column : column + 2 * HD] = jnp.dot(
                incoming[...], weights[:, column : column + 2 * HD], preferred_element_type=F32
            ).astype(BF16)
        for copy in more:
            copy.wait()
        spots = head_spots(seqs, length)
        each = [probs[number] for number in range(len(spots))]
        grad_probs = [dot_nt(grad_mixed[spot], values_here[spot]) for spot in spots]
        grad_values = [
            dot_tn(prob.astype(BF16), grad_mixed[spot]) for prob, spot in zip(each, spots)
        ]
        shifts = [
            jnp.sum(grad * prob, axis=-1, keepdims=True) for grad, prob in zip(grad_probs, each)
        ]
        grad_scores = [
            (prob * (grad - shift) * SCALE).astype(BF16)
            for prob, grad, shift in zip(each, grad_probs, shifts)
        ]
        grad_q = [
            jnp.dot(grad, keys_here[spot], preferred_element_type=F32)
            for grad, spot in zip(grad_scores, spots)
        ]
        grad_k = [dot_tn(grad, queries[spot]) for grad, spot in zip(grad_scores, spots)]
        for (rows, columns), one_q, one_k, one_v in zip(spots, grad_q, grad_k, grad_values):
            low = columns.start
            back = -sine[rows]
            grad_proj[rows, low : low + HD] = turn(one_q, cosine[rows], back).astype(BF16)
            low += WIDTH
            grad_proj[rows, low : low + HD] = turn(one_k, cosine[rows], back).astype(BF16)
            low += WIDTH
            grad_proj[rows, low : low + HD] = one_v.astype(BF16)


def inputs_back_kernel(places, chips, facts, incoming, previous, x, grad_proj, *rest):
    count = len(places)
    pieces = rest[:count]
    grad_inputs, weights, grad_normed, sems = rest[count:]

    @pl.when(facts[1] != 0)
    def _():
        copies = start_parts(pieces, places, chips, facts[0], weights, sems)
        x_f = x[...].astype(F32)
        inv_rms = rms_of(x_f)
        for part in range(3):
            for copy in copies[part]:
                copy.wait()
            taken = grad_proj[:, part * WIDTH : part * WIDTH + WIDTH]
            for low in range(0, x.shape[1], 256):
                product = dot_nt(taken, weights[part, low : low + 256, :])
                if part:
                    product = grad_normed[:, low : low + 256] + product
                grad_normed[:, low : low + 256] = product
        g_normed = grad_normed[...]
        shift = jnp.mean(g_normed * x_f, axis=-1, keepdims=True)
        grad_inputs[...] = (
            incoming[...].astype(F32) + inv_rms * g_normed - x_f * (inv_rms**3 * shift)
        ).astype(BF16)

    @pl.when(facts[1] == 0)
    def _():
        grad_inputs[...] = previous[...]


def far_offsets(chips):
    first = [chips // 2 - 1, chips // 2 + 1]
    return first, [offset for offset in range(chips) if offset not in first]


def term_kernel(chips, facts, incoming, mixed, mine_first, mine, others_first, others):
    me = facts[0]
    rows = incoming.shape[1] // (2 * chips)
    upper = lax.rem(me, 2) == 0
    targets = ((mine_first, others_first), (mine, others))
    for offsets, (target, other) in zip(far_offsets(chips), targets):
        for number, offset in enumerate(offsets):
            chip = chip_at(me, offset, chips)
            column = pl.multiple_of(chip * 2 * rows, 2 * rows)
            term = dot_tn(incoming[:, pl.ds(column, 2 * rows)], mixed[...])
            first, second = term[:rows], term[rows:]
            target[number] = jnp.where(upper, first, second).astype(BF16)
            other[number] = jnp.where(upper, second, first).astype(BF16)


def sum_rows(mine_first, mine, others_first, others, dp_count, tied):
    chips = dp_count // 2
    far = chips // 2
    ahead, behind = ring_pairs(chips, 1), ring_pairs(chips, -1)
    first, rest = far_offsets(chips)
    from_first, from_rest = swap_cores(others_first, dp_count), swap_cores(others, dp_count)
    up, down = (
        lax.ppermute((mine_first[side].astype(F32) + from_first[side].astype(F32)).astype(BF16), "dp", pairs)
        for side, pairs in enumerate((ahead, behind))
    )
    both = (mine.astype(F32) + from_rest.astype(F32)).astype(BF16)
    spot = rest.index(far)
    straight = (mine[spot].astype(F32) + from_rest[spot].astype(F32)).astype(BF16)
    both, straight, up, down = lax.optimization_barrier((both, straight, up, down))

    def held(offset):
        return both[rest.index(offset)].astype(F32)

    across = lax.ppermute(straight, "dp", ring_pairs(chips, far))
    for hop in range(far - 2, 0, -1):
        if hop == 1:
            up, down, tied = lax.optimization_barrier((up, down, tied))
        up = lax.ppermute((held(hop) + up.astype(F32)).astype(BF16), "dp", ahead)
        down = lax.ppermute((held(chips - hop) + down.astype(F32)).astype(BF16), "dp", behind)
    return held(0) + across.astype(F32) + up.astype(F32) + down.astype(F32), tied


def per_device(section_inputs, patch_index, w_qkv, w_out, out_cotangent):
    seqs, length, width = section_inputs.shape[1:]
    tokens = seqs * length
    sections = lax.axis_size("section")
    dp_count = lax.axis_size("dp")
    chips = dp_count // 2
    by_ring = dp_count % 4 == 0 and 4 <= chips <= 8
    dp_idx = lax.axis_index("dp").astype(jnp.int32)
    section_idx = lax.axis_index("section")
    x = section_inputs[0].reshape(tokens, width)
    shard = jnp.concatenate([w_qkv[0], w_out[0]], axis=1)
    if by_ring:
        pieces, places = gather_rows(shard, dp_count)
    else:
        pieces, places = [lax.all_gather(shard, "dp", axis=0, tiled=True)], [None]

    smem = pl.BlockSpec(memory_space=pltpu.SMEM)
    vmem = pl.BlockSpec(memory_space=pltpu.VMEM)
    anywhere = pl.BlockSpec(memory_space=pltpu.HBM)
    params = pltpu.CompilerParams(vmem_limit_bytes=VMEM_LIMIT)
    like = jax.ShapeDtypeStruct((tokens, width), BF16)
    heads_like = jax.ShapeDtypeStruct((tokens, WIDTH), BF16)

    table_like = jax.ShapeDtypeStruct((tokens, HD), F32)
    cosine, sine, queries, key_rows, values, probs, mixed = pl.pallas_call(
        functools.partial(forward_kernel, places, chips, seqs, length),
        out_shape=[table_like] * 2
        + [heads_like, pltpu.HBM((tokens, WIDTH), BF16), pltpu.HBM((tokens, WIDTH), BF16)]
        + [jax.ShapeDtypeStruct((HEADS * seqs, length, length), F32), heads_like],
        in_specs=[smem, vmem, vmem] + [anywhere] * len(pieces),
        out_specs=[vmem] * 7,
        scratch_shapes=[
            pltpu.VMEM((3, width, WIDTH), BF16),
            pltpu.VMEM((tokens, width), BF16),
            pltpu.SemaphoreType.DMA((3, len(pieces))),
        ],
        compiler_params=params,
        cost_estimate=pl.CostEstimate(
            flops=2 * tokens * width * 3 * WIDTH,
            bytes_accessed=6 * width * WIDTH,
            transcendentals=0,
        ),
        name="forward",
    )(jnp.stack([dp_idx, dp_idx]), x, patch_index, *pieces)
    key_rows, values = in_hbm(key_rows), in_hbm(values)
    mixed_above = lax.ppermute(mixed, "section", [(s, (s + 1) % sections) for s in range(sections)])

    def stage(number, incoming, previous):
        active = (section_idx == sections - 1 - number).astype(jnp.int32)
        facts = jnp.stack([dp_idx, active])
        grad_proj = pl.pallas_call(
            functools.partial(heads_back_kernel, places, chips, seqs, length),
            out_shape=jax.ShapeDtypeStruct((tokens, 3 * WIDTH), BF16),
            in_specs=[smem] + [vmem] * 4 + [anywhere] * 2 + [vmem] + [anywhere] * len(pieces),
            out_specs=vmem,
            scratch_shapes=[
                pltpu.VMEM((width, WIDTH), BF16),
                pltpu.VMEM((tokens, WIDTH), BF16),
                pltpu.VMEM((tokens, WIDTH), BF16),
                pltpu.VMEM((tokens, WIDTH), BF16),
                pltpu.SemaphoreType.DMA((len(pieces),)),
                pltpu.SemaphoreType.DMA((2,)),
            ],
            compiler_params=params,
            cost_estimate=pl.CostEstimate(
                flops=2 * tokens * width * WIDTH,
                bytes_accessed=8 * width * WIDTH,
                transcendentals=0,
            ),
            name="heads_back",
        )(facts, incoming, cosine, sine, queries, key_rows, values, probs, *pieces)
        return pl.pallas_call(
            functools.partial(inputs_back_kernel, places, chips),
            out_shape=like,
            in_specs=[smem] + [vmem] * 4 + [anywhere] * len(pieces),
            out_specs=vmem,
            scratch_shapes=[
                pltpu.VMEM((3, width, WIDTH), BF16),
                pltpu.VMEM((tokens, width), F32),
                pltpu.SemaphoreType.DMA((3, len(pieces))),
            ],
            compiler_params=params,
            cost_estimate=pl.CostEstimate(
                flops=2 * tokens * width * 3 * WIDTH,
                bytes_accessed=8 * width * WIDTH,
                transcendentals=0,
            ),
            name="inputs_back",
        )(facts, incoming, previous, x, grad_proj, *pieces)

    incoming = carried = out_cotangent.reshape(tokens, width)
    back = [(s, s - 1) for s in range(1, sections)]
    for number in range(sections - 1):
        carried = stage(number, incoming, carried)
        incoming = lax.ppermute(carried, "section", back)
    ready = carried

    if by_ring:
        first, rest = far_offsets(chips)
        mine_first, mine, others_first, others = pl.pallas_call(
            functools.partial(term_kernel, chips),
            out_shape=[
                jax.ShapeDtypeStruct((count, width // dp_count, WIDTH), BF16)
                for count in (len(first), len(rest)) * 2
            ],
            in_specs=[smem, vmem, vmem],
            out_specs=[vmem] * 4,
            compiler_params=params,
            cost_estimate=pl.CostEstimate(
                flops=2 * tokens * width * WIDTH,
                bytes_accessed=2 * width * WIDTH,
                transcendentals=0,
            ),
            name="term",
        )(jnp.stack([dp_idx, dp_idx]), ready, mixed_above)
        grad_sum, incoming = sum_rows(
            mine_first, mine, others_first, others, dp_count, incoming
        )
    else:
        grad_sum = lax.psum_scatter(
            dot_tn(ready, mixed_above), "dp", scatter_dimension=0, tiled=True
        )
    carried = stage(sections - 1, incoming, carried)
    grad_sum = lax.ppermute(
        grad_sum.astype(BF16), "section", [(s, (s - 1) % sections) for s in range(sections)]
    )
    grad_sum = grad_sum.astype(F32) * float(tokens * dp_count) ** (-0.5)
    return carried.reshape(1, seqs, length, width), grad_sum[None]


def solution(mesh):
    in_specs = (
        P("section", "dp", None, None),
        P("dp", None),
        P("section", "dp", None),
        P("section", "dp", None),
        P("dp", None, None),
    )
    out_specs = (P("section", "dp", None, None), P("section", "dp", None))
    return jax.shard_map(
        per_device, mesh=mesh, in_specs=in_specs, out_specs=out_specs, check_vma=False
    )
```

```python
import functools
import math

import jax
import jax.numpy as jnp
from jax import lax
from jax.experimental import pallas as pl
from jax.experimental.pallas import tpu as pltpu
from jax.sharding import PartitionSpec as P

HEADS = 8
HD = 128
GRID = 32
WIDTH = HEADS * HD
SCALE = HD**-0.5
F32 = jnp.float32
BF16 = jnp.bfloat16
VMEM_LIMIT = 28 * 1024 * 1024


def ring_pairs(chips, step):
    order = [2 * r if r < chips // 2 else 2 * (chips - 1 - r) + 1 for r in range(chips)]
    return [
        (2 * order[r] + core, 2 * order[(r + step) % chips] + core)
        for r in range(chips)
        for core in range(2)
    ]


def chip_at(me, offset, chips):
    chip = me // 2
    place = jnp.where(chip % 2 == 0, chip // 2, chips - 1 - chip // 2)
    there = (place + (offset + chips)) % chips
    return jnp.where(there < chips // 2, 2 * there, 2 * (chips - 1 - there) + 1)


def swap_cores(value, dp_count):
    return lax.ppermute(value, "dp", [(i, i ^ 1) for i in range(dp_count)])


def in_hbm(value):
    return pltpu.with_memory_space_constraint(value, pltpu.HBM)


def gather_rows(shard, dp_count):
    chips = dp_count // 2
    far = chips // 2
    half = shard.shape[0] // 2
    ahead, behind = ring_pairs(chips, 1), ring_pairs(chips, -1)
    up = down = shard
    pieces = [(shard, 0, 0, 0)]
    for hop in range(1, far):
        up = lax.ppermute(up, "dp", ahead)
        down = lax.ppermute(down, "dp", behind)
        pieces += [(up, -hop, 0, 0), (down, hop, 0, 0)]
    up = lax.ppermute(up[:half], "dp", ahead)
    down = lax.ppermute(down[half:], "dp", behind)
    pieces += [(up, -far, 0, 0), (down, far, 0, half)]
    pieces = [(in_hbm(value), *place) for value, *place in pieces]
    pieces += [
        (in_hbm(swap_cores(value, dp_count)), offset, 1, row) for value, offset, _, row in pieces
    ]
    return [piece[0] for piece in pieces], [piece[1:] for piece in pieces]


def start_rows(pieces, places, chips, me, columns, target, sem_at):
    copies = []
    per_owner = target.shape[0] // (2 * chips)
    for number, (piece, place) in enumerate(zip(pieces, places)):
        rows = piece.shape[0]
        into = target
        if place is not None:
            offset, other, low = place
            owner = 2 * chip_at(me, offset, chips) + lax.rem(me + other, 2)
            into = target.at[pl.ds(pl.multiple_of(owner * per_owner + low, rows), rows)]
        copy = pltpu.make_async_copy(piece.at[:, columns], into, sem_at(number))
        copy.start()
        copies.append(copy)
    return copies


def start_parts(pieces, places, chips, me, target, sems):
    return [
        start_rows(
            pieces, places, chips, me, pl.ds(part * WIDTH, WIDTH), target.at[part],
            lambda number, part=part: sems.at[part, number],
        )
        for part in range(3)
    ]


def head_spots(seqs, length):
    return [
        (slice(seq * length, seq * length + length), slice(head * HD, head * HD + HD))
        for head in range(HEADS)
        for seq in range(seqs)
    ]


def turn(value, cosine, sine):
    return value * cosine + pltpu.roll(value, HD // 2, 1) * sine


def rms_of(inputs_f):
    return lax.rsqrt(jnp.mean(inputs_f * inputs_f, axis=-1, keepdims=True) + 1e-06)


def dot_nt(a, b):
    return lax.dot_general(a, b, (((1,), (1,)), ((), ())), preferred_element_type=F32)


def dot_tn(a, b):
    return lax.dot_general(a, b, (((0,), (0,)), ((), ())), preferred_element_type=F32)


def rotation_tables(patch_index):
    length = patch_index.shape[1]
    lanes = lax.broadcasted_iota(jnp.int32, (length, HD), 1)
    slot = jnp.where(lanes < HD // 2, lanes, lanes - HD // 2)
    per_axis = (HD // 2 + 2) // 3
    spread = jnp.broadcast_to(patch_index.astype(F32), (HD, length))
    index = jnp.transpose(spread).astype(jnp.int32)
    place = jnp.where(
        slot % 3 == 0,
        index // (GRID * GRID),
        jnp.where(slot % 3 == 1, index // GRID % GRID, index % GRID),
    )
    rates = jnp.exp((slot // 3).astype(F32) * (-math.log(10000.0) / per_axis))
    angles = place.astype(F32) * rates
    sine = jnp.sin(angles)
    return jnp.cos(angles), jnp.where(lanes < HD // 2, -sine, sine)


def forward_kernel(places, chips, seqs, length, facts, x, patch_index, *rest):
    count = len(places)
    cosine, sine, queries, key_rows, values, probs, mixed, weights, normed, sems = rest[count:]
    copies = start_parts(rest[:count], places, chips, facts[0], weights, sems)
    x_f = x[...].astype(F32)
    normed[...] = (x_f * rms_of(x_f)).astype(BF16)
    for seq in range(seqs):
        rows = slice(seq * length, seq * length + length)
        cosine[rows], sine[rows] = rotation_tables(patch_index[seq : seq + 1])
    for part, target in enumerate((queries, key_rows, values)):
        for copy in copies[part]:
            copy.wait()
        for column in range(0, WIDTH, 4 * HD):
            block = jnp.dot(
                normed[...],
                weights[part, :, column : column + 4 * HD],
                preferred_element_type=F32,
            )
            for head in range(4):
                one = block[:, head * HD : head * HD + HD]
                if part < 2:
                    one = turn(one, cosine[...], sine[...])
                target[:, column + head * HD : column + head * HD + HD] = one.astype(BF16)
    spots = head_spots(seqs, length)
    scores = [dot_nt(queries[spot], key_rows[spot]) * SCALE for spot in spots]
    highest = [jnp.max(one, axis=-1, keepdims=True) for one in scores]
    raised = [jnp.exp(one - top) for one, top in zip(scores, highest)]
    totals = [jnp.sum(one, axis=-1, keepdims=True) for one in raised]
    each = [one * (1.0 / total) for one, total in zip(raised, totals)]
    for number, prob in enumerate(each):
        probs[number] = prob
    for spot, prob in zip(spots, each):
        mixed[spot] = jnp.dot(
            prob.astype(BF16), values[spot], preferred_element_type=F32
        ).astype(BF16)


def heads_back_kernel(
    places, chips, seqs, length,
    facts, incoming, cosine, sine, queries, key_rows, values, probs, *rest,
):
    count = len(places)
    pieces = rest[:count]
    grad_proj, weights, grad_mixed, keys_here, values_here, sems, more_sems = rest[count:]

    @pl.when(facts[1] != 0)
    def _():
        copies = start_rows(
            pieces, places, chips, facts[0], pl.ds(3 * WIDTH, WIDTH), weights,
            lambda number: sems.at[number],
        )
        more = [
            pltpu.make_async_copy(key_rows, keys_here, more_sems.at[0]),
            pltpu.make_async_copy(values, values_here, more_sems.at[1]),
        ]
        for copy in more:
            copy.start()
        for copy in copies:
            copy.wait()
        for column in range(0, WIDTH, 2 * HD):
            grad_mixed[:, column : column + 2 * HD] = jnp.dot(
                incoming[...], weights[:, column : column + 2 * HD], preferred_element_type=F32
            ).astype(BF16)
        for copy in more:
            copy.wait()
        spots = head_spots(seqs, length)
        each = [probs[number] for number in range(len(spots))]
        grad_probs = [dot_nt(grad_mixed[spot], values_here[spot]) for spot in spots]
        grad_values = [
            dot_tn(prob.astype(BF16), grad_mixed[spot]) for prob, spot in zip(each, spots)
        ]
        shifts = [
            jnp.sum(grad * prob, axis=-1, keepdims=True) for grad, prob in zip(grad_probs, each)
        ]
        grad_scores = [
            (prob * (grad - shift) * SCALE).astype(BF16)
            for prob, grad, shift in zip(each, grad_probs, shifts)
        ]
        grad_q = [
            jnp.dot(grad, keys_here[spot], preferred_element_type=F32)
            for grad, spot in zip(grad_scores, spots)
        ]
        grad_k = [dot_tn(grad, queries[spot]) for grad, spot in zip(grad_scores, spots)]
        for (rows, columns), one_q, one_k, one_v in zip(spots, grad_q, grad_k, grad_values):
            low = columns.start
            back = -sine[rows]
            grad_proj[rows, low : low + HD] = turn(one_q, cosine[rows], back).astype(BF16)
            low += WIDTH
            grad_proj[rows, low : low + HD] = turn(one_k, cosine[rows], back).astype(BF16)
            low += WIDTH
            grad_proj[rows, low : low + HD] = one_v.astype(BF16)


def inputs_back_kernel(places, chips, facts, incoming, previous, x, grad_proj, *rest):
    count = len(places)
    pieces = rest[:count]
    grad_inputs, weights, grad_normed, sems = rest[count:]

    @pl.when(facts[1] != 0)
    def _():
        copies = start_parts(pieces, places, chips, facts[0], weights, sems)
        x_f = x[...].astype(F32)
        inv_rms = rms_of(x_f)
        for part in range(3):
            for copy in copies[part]:
                copy.wait()
            taken = grad_proj[:, part * WIDTH : part * WIDTH + WIDTH]
            for low in range(0, x.shape[1], 256):
                product = dot_nt(taken, weights[part, low : low + 256, :])
                if part:
                    product = grad_normed[:, low : low + 256] + product
                grad_normed[:, low : low + 256] = product
        g_normed = grad_normed[...]
        shift = jnp.mean(g_normed * x_f, axis=-1, keepdims=True)
        grad_inputs[...] = (
            incoming[...].astype(F32) + inv_rms * g_normed - x_f * (inv_rms**3 * shift)
        ).astype(BF16)

    @pl.when(facts[1] == 0)
    def _():
        grad_inputs[...] = previous[...]


def far_offsets(chips):
    first = [chips // 2 - 1, chips // 2 + 1]
    return first, [offset for offset in range(chips) if offset not in first]


def term_kernel(chips, facts, incoming, mixed, mine_first, mine, others_first, others):
    me = facts[0]
    rows = incoming.shape[1] // (2 * chips)
    upper = lax.rem(me, 2) == 0
    targets = ((mine_first, others_first), (mine, others))
    for offsets, (target, other) in zip(far_offsets(chips), targets):
        columns = [
            pl.ds(pl.multiple_of(chip_at(me, offset, chips) * 2 * rows, 2 * rows), 2 * rows)
            for offset in offsets
        ]
        taken = jnp.concatenate([incoming[:, column] for column in columns], axis=1)
        term = dot_tn(taken, mixed[...])
        for number in range(len(offsets)):
            low = number * 2 * rows
            first, second = term[low : low + rows], term[low + rows : low + 2 * rows]
            target[number] = jnp.where(upper, first, second).astype(BF16)
            other[number] = jnp.where(upper, second, first).astype(BF16)


def sum_rows(mine_first, mine, others_first, others, dp_count, tied):
    chips = dp_count // 2
    far = chips // 2
    ahead, behind = ring_pairs(chips, 1), ring_pairs(chips, -1)
    first, rest = far_offsets(chips)
    from_first, from_rest = swap_cores(others_first, dp_count), swap_cores(others, dp_count)
    up, down = (
        lax.ppermute((mine_first[side].astype(F32) + from_first[side].astype(F32)).astype(BF16), "dp", pairs)
        for side, pairs in enumerate((ahead, behind))
    )
    both = (mine.astype(F32) + from_rest.astype(F32)).astype(BF16)
    spot = rest.index(far)
    straight = (mine[spot].astype(F32) + from_rest[spot].astype(F32)).astype(BF16)
    both, straight, up, down = lax.optimization_barrier((both, straight, up, down))

    def held(offset):
        return both[rest.index(offset)].astype(F32)

    across = lax.ppermute(straight, "dp", ring_pairs(chips, far))
    for hop in range(far - 2, 0, -1):
        if hop == 1:
            up, down, tied = lax.optimization_barrier((up, down, tied))
        up = lax.ppermute((held(hop) + up.astype(F32)).astype(BF16), "dp", ahead)
        down = lax.ppermute((held(chips - hop) + down.astype(F32)).astype(BF16), "dp", behind)
    return held(0) + across.astype(F32) + up.astype(F32) + down.astype(F32), tied


def per_device(section_inputs, patch_index, w_qkv, w_out, out_cotangent):
    seqs, length, width = section_inputs.shape[1:]
    tokens = seqs * length
    sections = lax.axis_size("section")
    dp_count = lax.axis_size("dp")
    chips = dp_count // 2
    by_ring = dp_count % 4 == 0 and 4 <= chips <= 8
    dp_idx = lax.axis_index("dp").astype(jnp.int32)
    section_idx = lax.axis_index("section")
    x = section_inputs[0].reshape(tokens, width)
    shard = jnp.concatenate([w_qkv[0], w_out[0]], axis=1)
    if by_ring:
        pieces, places = gather_rows(shard, dp_count)
    else:
        pieces, places = [lax.all_gather(shard, "dp", axis=0, tiled=True)], [None]

    smem = pl.BlockSpec(memory_space=pltpu.SMEM)
    vmem = pl.BlockSpec(memory_space=pltpu.VMEM)
    anywhere = pl.BlockSpec(memory_space=pltpu.HBM)
    params = pltpu.CompilerParams(vmem_limit_bytes=VMEM_LIMIT)
    like = jax.ShapeDtypeStruct((tokens, width), BF16)
    heads_like = jax.ShapeDtypeStruct((tokens, WIDTH), BF16)

    table_like = jax.ShapeDtypeStruct((tokens, HD), F32)
    cosine, sine, queries, key_rows, values, probs, mixed = pl.pallas_call(
        functools.partial(forward_kernel, places, chips, seqs, length),
        out_shape=[table_like] * 2
        + [heads_like, pltpu.HBM((tokens, WIDTH), BF16), pltpu.HBM((tokens, WIDTH), BF16)]
        + [jax.ShapeDtypeStruct((HEADS * seqs, length, length), F32), heads_like],
        in_specs=[smem, vmem, vmem] + [anywhere] * len(pieces),
        out_specs=[vmem] * 7,
        scratch_shapes=[
            pltpu.VMEM((3, width, WIDTH), BF16),
            pltpu.VMEM((tokens, width), BF16),
            pltpu.SemaphoreType.DMA((3, len(pieces))),
        ],
        compiler_params=params,
        cost_estimate=pl.CostEstimate(
            flops=2 * tokens * width * 3 * WIDTH,
            bytes_accessed=6 * width * WIDTH,
            transcendentals=0,
        ),
        name="forward",
    )(jnp.stack([dp_idx, dp_idx]), x, patch_index, *pieces)
    key_rows, values = in_hbm(key_rows), in_hbm(values)
    mixed_above = lax.ppermute(mixed, "section", [(s, (s + 1) % sections) for s in range(sections)])

    def stage(number, incoming, previous):
        active = (section_idx == sections - 1 - number).astype(jnp.int32)
        facts = jnp.stack([dp_idx, active])
        grad_proj = pl.pallas_call(
            functools.partial(heads_back_kernel, places, chips, seqs, length),
            out_shape=jax.ShapeDtypeStruct((tokens, 3 * WIDTH), BF16),
            in_specs=[smem] + [vmem] * 4 + [anywhere] * 2 + [vmem] + [anywhere] * len(pieces),
            out_specs=vmem,
            scratch_shapes=[
                pltpu.VMEM((width, WIDTH), BF16),
                pltpu.VMEM((tokens, WIDTH), BF16),
                pltpu.VMEM((tokens, WIDTH), BF16),
                pltpu.VMEM((tokens, WIDTH), BF16),
                pltpu.SemaphoreType.DMA((len(pieces),)),
                pltpu.SemaphoreType.DMA((2,)),
            ],
            compiler_params=params,
            cost_estimate=pl.CostEstimate(
                flops=2 * tokens * width * WIDTH,
                bytes_accessed=8 * width * WIDTH,
                transcendentals=0,
            ),
            name="heads_back",
        )(facts, incoming, cosine, sine, queries, key_rows, values, probs, *pieces)
        return pl.pallas_call(
            functools.partial(inputs_back_kernel, places, chips),
            out_shape=like,
            in_specs=[smem] + [vmem] * 4 + [anywhere] * len(pieces),
            out_specs=vmem,
            scratch_shapes=[
                pltpu.VMEM((3, width, WIDTH), BF16),
                pltpu.VMEM((tokens, width), F32),
                pltpu.SemaphoreType.DMA((3, len(pieces))),
            ],
            compiler_params=params,
            cost_estimate=pl.CostEstimate(
                flops=2 * tokens * width * 3 * WIDTH,
                bytes_accessed=8 * width * WIDTH,
                transcendentals=0,
            ),
            name="inputs_back",
        )(facts, incoming, previous, x, grad_proj, *pieces)

    incoming = carried = out_cotangent.reshape(tokens, width)
    back = [(s, s - 1) for s in range(1, sections)]
    for number in range(sections - 1):
        carried = stage(number, incoming, carried)
        incoming = lax.ppermute(carried, "section", back)
    ready = carried

    if by_ring:
        first, rest = far_offsets(chips)
        mine_first, mine, others_first, others = pl.pallas_call(
            functools.partial(term_kernel, chips),
            out_shape=[
                jax.ShapeDtypeStruct((count, width // dp_count, WIDTH), BF16)
                for count in (len(first), len(rest)) * 2
            ],
            in_specs=[smem, vmem, vmem],
            out_specs=[vmem] * 4,
            compiler_params=params,
            cost_estimate=pl.CostEstimate(
                flops=2 * tokens * width * WIDTH,
                bytes_accessed=2 * width * WIDTH,
                transcendentals=0,
            ),
            name="term",
        )(jnp.stack([dp_idx, dp_idx]), ready, mixed_above)
        grad_sum, incoming = sum_rows(
            mine_first, mine, others_first, others, dp_count, incoming
        )
    else:
        grad_sum = lax.psum_scatter(
            dot_tn(ready, mixed_above), "dp", scatter_dimension=0, tiled=True
        )
    carried = stage(sections - 1, incoming, carried)
    grad_sum = lax.ppermute(
        grad_sum.astype(BF16), "section", [(s, (s - 1) % sections) for s in range(sections)]
    )
    grad_sum = grad_sum.astype(F32) * float(tokens * dp_count) ** (-0.5)
    return carried.reshape(1, seqs, length, width), grad_sum[None]


def solution(mesh):
    in_specs = (
        P("section", "dp", None, None),
        P("dp", None),
        P("section", "dp", None),
        P("section", "dp", None),
        P("dp", None, None),
    )
    out_specs = (P("section", "dp", None, None), P("section", "dp", None))
    return jax.shard_map(
        per_device, mesh=mesh, in_specs=in_specs, out_specs=out_specs, check_vma=False
    )
```

```python
import functools
import math

import jax
import jax.numpy as jnp
from jax import lax
from jax.experimental import pallas as pl
from jax.experimental.pallas import tpu as pltpu
from jax.sharding import PartitionSpec as P

HEADS = 8
HD = 128
GRID = 32
WIDTH = HEADS * HD
SCALE = HD**-0.5
F32 = jnp.float32
BF16 = jnp.bfloat16
VMEM_LIMIT = 28 * 1024 * 1024


def ring_pairs(chips, step):
    order = [2 * r if r < chips // 2 else 2 * (chips - 1 - r) + 1 for r in range(chips)]
    return [
        (2 * order[r] + core, 2 * order[(r + step) % chips] + core)
        for r in range(chips)
        for core in range(2)
    ]


def chip_at(me, offset, chips):
    chip = me // 2
    place = jnp.where(chip % 2 == 0, chip // 2, chips - 1 - chip // 2)
    there = (place + (offset + chips)) % chips
    return jnp.where(there < chips // 2, 2 * there, 2 * (chips - 1 - there) + 1)


def swap_cores(value, dp_count):
    return lax.ppermute(value, "dp", [(i, i ^ 1) for i in range(dp_count)])


def in_hbm(value):
    return pltpu.with_memory_space_constraint(value, pltpu.HBM)


def gather_rows(shard, dp_count):
    chips = dp_count // 2
    far = chips // 2
    half = shard.shape[0] // 2
    ahead, behind = ring_pairs(chips, 1), ring_pairs(chips, -1)
    up = down = shard
    pieces = [(shard, 0, 0, 0)]
    for hop in range(1, far):
        up = lax.ppermute(up, "dp", ahead)
        down = lax.ppermute(down, "dp", behind)
        pieces += [(up, -hop, 0, 0), (down, hop, 0, 0)]
    up = lax.ppermute(up[:half], "dp", ahead)
    down = lax.ppermute(down[half:], "dp", behind)
    pieces += [(up, -far, 0, 0), (down, far, 0, half)]
    pieces = [(in_hbm(value), *place) for value, *place in pieces]
    pieces += [
        (in_hbm(swap_cores(value, dp_count)), offset, 1, row) for value, offset, _, row in pieces
    ]
    return [piece[0] for piece in pieces], [piece[1:] for piece in pieces]


def start_rows(pieces, places, chips, me, columns, target, sem_at):
    copies = []
    per_owner = target.shape[0] // (2 * chips)
    for number, (piece, place) in enumerate(zip(pieces, places)):
        rows = piece.shape[0]
        into = target
        if place is not None:
            offset, other, low = place
            owner = 2 * chip_at(me, offset, chips) + lax.rem(me + other, 2)
            into = target.at[pl.ds(pl.multiple_of(owner * per_owner + low, rows), rows)]
        copy = pltpu.make_async_copy(piece.at[:, columns], into, sem_at(number))
        copy.start()
        copies.append(copy)
    return copies


def start_parts(pieces, places, chips, me, target, sems):
    return [
        start_rows(
            pieces, places, chips, me, pl.ds(part * WIDTH, WIDTH), target.at[part],
            lambda number, part=part: sems.at[part, number],
        )
        for part in range(3)
    ]


def head_spots(seqs, length):
    return [
        (slice(seq * length, seq * length + length), slice(head * HD, head * HD + HD))
        for head in range(HEADS)
        for seq in range(seqs)
    ]


def turn(value, cosine, sine):
    return value * cosine + pltpu.roll(value, HD // 2, 1) * sine


def rms_of(inputs_f):
    return lax.rsqrt(jnp.mean(inputs_f * inputs_f, axis=-1, keepdims=True) + 1e-06)


def dot_nt(a, b):
    return lax.dot_general(a, b, (((1,), (1,)), ((), ())), preferred_element_type=F32)


def dot_tn(a, b):
    return lax.dot_general(a, b, (((0,), (0,)), ((), ())), preferred_element_type=F32)


def rotation_tables(patch_index):
    length = patch_index.shape[1]
    lanes = lax.broadcasted_iota(jnp.int32, (length, HD), 1)
    slot = jnp.where(lanes < HD // 2, lanes, lanes - HD // 2)
    per_axis = (HD // 2 + 2) // 3
    spread = jnp.broadcast_to(patch_index.astype(F32), (HD, length))
    index = jnp.transpose(spread).astype(jnp.int32)
    place = jnp.where(
        slot % 3 == 0,
        index // (GRID * GRID),
        jnp.where(slot % 3 == 1, index // GRID % GRID, index % GRID),
    )
    rates = jnp.exp((slot // 3).astype(F32) * (-math.log(10000.0) / per_axis))
    angles = place.astype(F32) * rates
    sine = jnp.sin(angles)
    return jnp.cos(angles), jnp.where(lanes < HD // 2, -sine, sine)


def forward_kernel(places, chips, seqs, length, facts, x, patch_index, *rest):
    count = len(places)
    cosine, sine, queries, key_rows, values, probs, mixed, weights, normed, sems = rest[count:]
    copies = start_parts(rest[:count], places, chips, facts[0], weights, sems)
    x_f = x[...].astype(F32)
    normed[...] = (x_f * rms_of(x_f)).astype(BF16)
    for seq in range(seqs):
        rows = slice(seq * length, seq * length + length)
        cosine[rows], sine[rows] = rotation_tables(patch_index[seq : seq + 1])
    for part, target in enumerate((queries, key_rows, values)):
        for copy in copies[part]:
            copy.wait()
        for column in range(0, WIDTH, 4 * HD):
            block = jnp.dot(
                normed[...],
                weights[part, :, column : column + 4 * HD],
                preferred_element_type=F32,
            )
            for head in range(4):
                one = block[:, head * HD : head * HD + HD]
                if part < 2:
                    one = turn(one, cosine[...], sine[...])
                target[:, column + head * HD : column + head * HD + HD] = one.astype(BF16)
    spots = head_spots(seqs, length)
    scores = [dot_nt(queries[spot], key_rows[spot]) * SCALE for spot in spots]
    highest = [jnp.max(one, axis=-1, keepdims=True) for one in scores]
    raised = [jnp.exp(one - top) for one, top in zip(scores, highest)]
    totals = [jnp.sum(one, axis=-1, keepdims=True) for one in raised]
    each = [one * (1.0 / total) for one, total in zip(raised, totals)]
    for number, prob in enumerate(each):
        probs[number] = prob
    for spot, prob in zip(spots, each):
        mixed[spot] = jnp.dot(
            prob.astype(BF16), values[spot], preferred_element_type=F32
        ).astype(BF16)


def heads_back_kernel(
    places, chips, seqs, length,
    facts, incoming, cosine, sine, queries, key_rows, values, probs, *rest,
):
    count = len(places)
    pieces = rest[:count]
    grad_proj, weights, grad_mixed, keys_here, values_here, sems, more_sems = rest[count:]

    @pl.when(facts[1] != 0)
    def _():
        copies = start_rows(
            pieces, places, chips, facts[0], pl.ds(3 * WIDTH, WIDTH), weights,
            lambda number: sems.at[number],
        )
        more = [
            pltpu.make_async_copy(key_rows, keys_here, more_sems.at[0]),
            pltpu.make_async_copy(values, values_here, more_sems.at[1]),
        ]
        for copy in more:
            copy.start()
        for copy in copies:
            copy.wait()
        for column in range(0, WIDTH, 4 * HD):
            grad_mixed[:, column : column + 4 * HD] = jnp.dot(
                incoming[...], weights[:, column : column + 4 * HD], preferred_element_type=F32
            ).astype(BF16)
        for copy in more:
            copy.wait()
        spots = head_spots(seqs, length)
        each = [probs[number] for number in range(len(spots))]
        grad_probs = [dot_nt(grad_mixed[spot], values_here[spot]) for spot in spots]
        grad_values = [
            dot_tn(prob.astype(BF16), grad_mixed[spot]) for prob, spot in zip(each, spots)
        ]
        shifts = [
            jnp.sum(grad * prob, axis=-1, keepdims=True) for grad, prob in zip(grad_probs, each)
        ]
        grad_scores = [
            (prob * (grad - shift) * SCALE).astype(BF16)
            for prob, grad, shift in zip(each, grad_probs, shifts)
        ]
        grad_q = [
            jnp.dot(grad, keys_here[spot], preferred_element_type=F32)
            for grad, spot in zip(grad_scores, spots)
        ]
        grad_k = [dot_tn(grad, queries[spot]) for grad, spot in zip(grad_scores, spots)]
        for (rows, columns), one_q, one_k, one_v in zip(spots, grad_q, grad_k, grad_values):
            low = columns.start
            back = -sine[rows]
            grad_proj[rows, low : low + HD] = turn(one_q, cosine[rows], back).astype(BF16)
            low += WIDTH
            grad_proj[rows, low : low + HD] = turn(one_k, cosine[rows], back).astype(BF16)
            low += WIDTH
            grad_proj[rows, low : low + HD] = one_v.astype(BF16)


def inputs_back_kernel(places, chips, facts, incoming, previous, x, grad_proj, *rest):
    count = len(places)
    pieces = rest[:count]
    grad_inputs, weights, grad_normed, sems = rest[count:]

    @pl.when(facts[1] != 0)
    def _():
        copies = start_parts(pieces, places, chips, facts[0], weights, sems)
        x_f = x[...].astype(F32)
        inv_rms = rms_of(x_f)
        for part in range(3):
            for copy in copies[part]:
                copy.wait()
            taken = grad_proj[:, part * WIDTH : part * WIDTH + WIDTH]
            for low in range(0, x.shape[1], 512):
                product = dot_nt(taken, weights[part, low : low + 512, :])
                if part:
                    product = grad_normed[:, low : low + 512] + product
                grad_normed[:, low : low + 512] = product
        g_normed = grad_normed[...]
        shift = jnp.mean(g_normed * x_f, axis=-1, keepdims=True)
        grad_inputs[...] = (
            incoming[...].astype(F32) + inv_rms * g_normed - x_f * (inv_rms**3 * shift)
        ).astype(BF16)

    @pl.when(facts[1] == 0)
    def _():
        grad_inputs[...] = previous[...]


def far_offsets(chips):
    first = [chips // 2 - 1, chips // 2 + 1]
    return first, [offset for offset in range(chips) if offset not in first]


def term_kernel(chips, facts, incoming, mixed, mine_first, mine, others_first, others):
    me = facts[0]
    rows = incoming.shape[1] // (2 * chips)
    upper = lax.rem(me, 2) == 0
    targets = ((mine_first, others_first), (mine, others))
    for offsets, (target, other) in zip(far_offsets(chips), targets):
        for number, offset in enumerate(offsets):
            chip = chip_at(me, offset, chips)
            column = pl.multiple_of(chip * 2 * rows, 2 * rows)
            term = dot_tn(incoming[:, pl.ds(column, 2 * rows)], mixed[...])
            first, second = term[:rows], term[rows:]
            target[number] = jnp.where(upper, first, second).astype(BF16)
            other[number] = jnp.where(upper, second, first).astype(BF16)


def sum_rows(mine_first, mine, others_first, others, dp_count, tied):
    chips = dp_count // 2
    far = chips // 2
    ahead, behind = ring_pairs(chips, 1), ring_pairs(chips, -1)
    first, rest = far_offsets(chips)
    from_first, from_rest = swap_cores(others_first, dp_count), swap_cores(others, dp_count)
    up, down = (
        lax.ppermute((mine_first[side].astype(F32) + from_first[side].astype(F32)).astype(BF16), "dp", pairs)
        for side, pairs in enumerate((ahead, behind))
    )
    both = (mine.astype(F32) + from_rest.astype(F32)).astype(BF16)
    spot = rest.index(far)
    straight = (mine[spot].astype(F32) + from_rest[spot].astype(F32)).astype(BF16)
    both, straight, up, down = lax.optimization_barrier((both, straight, up, down))

    def held(offset):
        return both[rest.index(offset)].astype(F32)

    across = lax.ppermute(straight, "dp", ring_pairs(chips, far))
    for hop in range(far - 2, 0, -1):
        if hop == 1:
            up, down, tied = lax.optimization_barrier((up, down, tied))
        up = lax.ppermute((held(hop) + up.astype(F32)).astype(BF16), "dp", ahead)
        down = lax.ppermute((held(chips - hop) + down.astype(F32)).astype(BF16), "dp", behind)
    return held(0) + across.astype(F32) + up.astype(F32) + down.astype(F32), tied


def per_device(section_inputs, patch_index, w_qkv, w_out, out_cotangent):
    seqs, length, width = section_inputs.shape[1:]
    tokens = seqs * length
    sections = lax.axis_size("section")
    dp_count = lax.axis_size("dp")
    chips = dp_count // 2
    by_ring = dp_count % 4 == 0 and 4 <= chips <= 8
    dp_idx = lax.axis_index("dp").astype(jnp.int32)
    section_idx = lax.axis_index("section")
    x = section_inputs[0].reshape(tokens, width)
    shard = jnp.concatenate([w_qkv[0], w_out[0]], axis=1)
    if by_ring:
        pieces, places = gather_rows(shard, dp_count)
    else:
        pieces, places = [lax.all_gather(shard, "dp", axis=0, tiled=True)], [None]

    smem = pl.BlockSpec(memory_space=pltpu.SMEM)
    vmem = pl.BlockSpec(memory_space=pltpu.VMEM)
    anywhere = pl.BlockSpec(memory_space=pltpu.HBM)
    params = pltpu.CompilerParams(vmem_limit_bytes=VMEM_LIMIT)
    like = jax.ShapeDtypeStruct((tokens, width), BF16)
    heads_like = jax.ShapeDtypeStruct((tokens, WIDTH), BF16)

    table_like = jax.ShapeDtypeStruct((tokens, HD), F32)
    cosine, sine, queries, key_rows, values, probs, mixed = pl.pallas_call(
        functools.partial(forward_kernel, places, chips, seqs, length),
        out_shape=[table_like] * 2
        + [heads_like, pltpu.HBM((tokens, WIDTH), BF16), pltpu.HBM((tokens, WIDTH), BF16)]
        + [jax.ShapeDtypeStruct((HEADS * seqs, length, length), F32), heads_like],
        in_specs=[smem, vmem, vmem] + [anywhere] * len(pieces),
        out_specs=[vmem] * 7,
        scratch_shapes=[
            pltpu.VMEM((3, width, WIDTH), BF16),
            pltpu.VMEM((tokens, width), BF16),
            pltpu.SemaphoreType.DMA((3, len(pieces))),
        ],
        compiler_params=params,
        cost_estimate=pl.CostEstimate(
            flops=2 * tokens * width * 3 * WIDTH,
            bytes_accessed=6 * width * WIDTH,
            transcendentals=0,
        ),
        name="forward",
    )(jnp.stack([dp_idx, dp_idx]), x, patch_index, *pieces)
    key_rows, values = in_hbm(key_rows), in_hbm(values)
    mixed_above = lax.ppermute(mixed, "section", [(s, (s + 1) % sections) for s in range(sections)])

    def stage(number, incoming, previous):
        active = (section_idx == sections - 1 - number).astype(jnp.int32)
        facts = jnp.stack([dp_idx, active])
        grad_proj = pl.pallas_call(
            functools.partial(heads_back_kernel, places, chips, seqs, length),
            out_shape=jax.ShapeDtypeStruct((tokens, 3 * WIDTH), BF16),
            in_specs=[smem] + [vmem] * 4 + [anywhere] * 2 + [vmem] + [anywhere] * len(pieces),
            out_specs=vmem,
            scratch_shapes=[
                pltpu.VMEM((width, WIDTH), BF16),
                pltpu.VMEM((tokens, WIDTH), BF16),
                pltpu.VMEM((tokens, WIDTH), BF16),
                pltpu.VMEM((tokens, WIDTH), BF16),
                pltpu.SemaphoreType.DMA((len(pieces),)),
                pltpu.SemaphoreType.DMA((2,)),
            ],
            compiler_params=params,
            cost_estimate=pl.CostEstimate(
                flops=2 * tokens * width * WIDTH,
                bytes_accessed=8 * width * WIDTH,
                transcendentals=0,
            ),
            name="heads_back",
        )(facts, incoming, cosine, sine, queries, key_rows, values, probs, *pieces)
        return pl.pallas_call(
            functools.partial(inputs_back_kernel, places, chips),
            out_shape=like,
            in_specs=[smem] + [vmem] * 4 + [anywhere] * len(pieces),
            out_specs=vmem,
            scratch_shapes=[
                pltpu.VMEM((3, width, WIDTH), BF16),
                pltpu.VMEM((tokens, width), F32),
                pltpu.SemaphoreType.DMA((3, len(pieces))),
            ],
            compiler_params=params,
            cost_estimate=pl.CostEstimate(
                flops=2 * tokens * width * 3 * WIDTH,
                bytes_accessed=8 * width * WIDTH,
                transcendentals=0,
            ),
            name="inputs_back",
        )(facts, incoming, previous, x, grad_proj, *pieces)

    incoming = carried = out_cotangent.reshape(tokens, width)
    back = [(s, s - 1) for s in range(1, sections)]
    for number in range(sections - 1):
        carried = stage(number, incoming, carried)
        incoming = lax.ppermute(carried, "section", back)
    ready = carried

    if by_ring:
        first, rest = far_offsets(chips)
        mine_first, mine, others_first, others = pl.pallas_call(
            functools.partial(term_kernel, chips),
            out_shape=[
                jax.ShapeDtypeStruct((count, width // dp_count, WIDTH), BF16)
                for count in (len(first), len(rest)) * 2
            ],
            in_specs=[smem, vmem, vmem],
            out_specs=[vmem] * 4,
            compiler_params=params,
            cost_estimate=pl.CostEstimate(
                flops=2 * tokens * width * WIDTH,
                bytes_accessed=2 * width * WIDTH,
                transcendentals=0,
            ),
            name="term",
        )(jnp.stack([dp_idx, dp_idx]), ready, mixed_above)
        grad_sum, incoming = sum_rows(
            mine_first, mine, others_first, others, dp_count, incoming
        )
    else:
        grad_sum = lax.psum_scatter(
            dot_tn(ready, mixed_above), "dp", scatter_dimension=0, tiled=True
        )
    carried = stage(sections - 1, incoming, carried)
    grad_sum = lax.ppermute(
        grad_sum.astype(BF16), "section", [(s, (s - 1) % sections) for s in range(sections)]
    )
    grad_sum = grad_sum.astype(F32) * float(tokens * dp_count) ** (-0.5)
    return carried.reshape(1, seqs, length, width), grad_sum[None]


def solution(mesh):
    in_specs = (
        P("section", "dp", None, None),
        P("dp", None),
        P("section", "dp", None),
        P("section", "dp", None),
        P("dp", None, None),
    )
    out_specs = (P("section", "dp", None, None), P("section", "dp", None))
    return jax.shard_map(
        per_device, mesh=mesh, in_specs=in_specs, out_specs=out_specs, check_vma=False
    )
```
